512 devices in a mesh: band: 128 (over y, z, core), det: 4 (over x).
Axes of the slice: x: 4, y: 8, z: 8, core: 2. Of those that a mesh axis runs over, the one named last changes fastest.
Arguments:
- sky_coeffs: float32 [3, 2, 128, 2048], P(None, None, 'band', 'det'), may hold values from -6 to 6
- beam_coeffs: bfloat16 [4, 3, 2, 17, 2048], P('det'), may hold values from -2.5 to 2.5
- wigner_panel: bfloat16 [128, 17, 2048, 128], P('band', None, 'det'), may hold values from -0.125 to 0.125
- m_values: int32 [128], replicated, may hold values from 0 to 4095, as said below
- cycle_table: int32 [128, 3], replicated, may hold values from -1 to 127, as said below
- send_lists: int32 [4, 128, 128, 2], P('det'), may hold values from -1 to 12287, as said below
- sample_block: int32 [4, 524288], P('det', 'band'), may hold values from 0 to 255, as said below
- sample_phi: int32 [4, 524288], P('det', 'band'), may hold values from 0 to 126
- sample_psi: int32 [4, 524288], P('det', 'band'), may hold values from 0 to 31
- sample_frac: float32 [2, 4, 524288], P(None, 'det', 'band'), may hold values from 0 to 1
Outputs:
- timestream: float32 [4, 524288], P('det', 'band')
The draws below stay inside these ranges and needn't reach their ends.
Inputs may be any that keep to these rules, and one draw needn't show every extreme that they name: `cycle_table`: each cycle stands in exactly one slot; -1 marks an empty slot; some cycle band fills all 3 slots, many hold none. `send_lists`: of one detector's entries from all bands to one owner, at most 8 are not -1, and every owner reaches 8; an entry from a band that holds no cycle is -1; an entry that is not -1 is slot * 4096 + start, with slot a filled slot of band src and start the block's first phi cell. `sample_block`: src * 2 + entry of an entry that is not -1 in the detector's list from band src to the sample's owner. `m_values`: distinct orders; 0 and 4095 among them.
All inputs are finite; a program needn't handle non-finite values.
Results may differ from the reference program's by a relative error of at most 0.0051.
Values may be sent and summed in bfloat16 or wider, within the bound.
A program may use at most 64 MiB of HBM per device.

```python
import math
import jax
import jax.numpy as jnp
from jax import lax

COMP = 3
L = 2048
LMAX = 4096
BMAX = 8
MPRIME = 17
NPSI = 32
NPHI = 4096
M_ALL = 128
NDET = 4
CYCLES = 128
CYCLE_SLOTS = 3
LIST_LEN = 2
LISTED = 8
BLOCK_PHI = 128
S_DEV = 4096
NSAMP = 524288
N_BAND = 128


def cycle_layout(key):
    base = jax.random.fold_in(key, 7)
    first_key, second_key, third_key = jax.random.split(base, 3)
    middle = (jax.random.permutation(first_key, N_BAND - 2) + 1).astype(jnp.int32)
    full_band = middle[0]
    extra_band = middle[1]
    cycle_order = jax.random.permutation(second_key, CYCLES).astype(jnp.int32)
    total = N_BAND * CYCLE_SLOTS
    slot_ids = jnp.arange(total, dtype=jnp.int32)
    slot_band = slot_ids // CYCLE_SLOTS
    slot_place = slot_ids % CYCLE_SLOTS
    shuffled = jax.random.permutation(third_key, total).astype(jnp.int32)
    opener = (slot_place == 0) & ((slot_band == 0) | (slot_band == N_BAND - 1) | (slot_band == extra_band))
    priority = jnp.where((slot_band == full_band) | opener, shuffled - total, shuffled)
    chosen = jnp.argsort(priority)[:CYCLES]
    table = jnp.full((total,), -1, jnp.int32).at[chosen].set(cycle_order)
    return table.reshape(N_BAND, CYCLE_SLOTS)


def listing(key):
    table = cycle_layout(key)
    filled = table >= 0
    counts = jnp.sum(filled.astype(jnp.int32), 1)
    first_slot = jnp.argmax(filled.astype(jnp.int32), 1).astype(jnp.int32)
    slot_key, start_key, pick_key = jax.random.split(jax.random.fold_in(key, 19), 3)
    shape = (NDET, N_BAND, N_BAND, LIST_LEN)
    wanted = jax.random.randint(slot_key, shape, 0, CYCLE_SLOTS)
    sources = jnp.broadcast_to(jnp.arange(N_BAND, dtype=jnp.int32)[None, :, None, None], shape)
    slot_index = jnp.where(filled[sources, wanted], wanted, first_slot[sources])
    starts = jax.random.randint(start_key, shape, 0, NPHI)
    codes = (slot_index * NPHI + starts).astype(jnp.int32)
    entry_count = N_BAND * LIST_LEN
    valid = jnp.transpose(counts[sources] > 0, (0, 2, 1, 3)).reshape(NDET, N_BAND, entry_count)
    entry_ids = jnp.arange(entry_count, dtype=jnp.int32)
    scores = jax.random.randint(pick_key, (NDET, N_BAND, entry_count), 0, 2 ** 20) * entry_count + entry_ids[None, None, :]
    full = jnp.argmax(counts).astype(jnp.int32)
    scores = scores.at[0, 0, full * LIST_LEN].set(-3)
    scores = scores.at[0, 0, 0].set(-2)
    scores = scores.at[0, 0, entry_count - 1].set(-1)
    keyed = jnp.where(valid, scores, scores + 2 ** 29)
    order = jnp.argsort(keyed, axis=-1).astype(jnp.int32)
    rank = jnp.argsort(order, axis=-1).astype(jnp.int32)
    picked = rank < LISTED
    listed = jnp.transpose(picked.reshape(NDET, N_BAND, N_BAND, LIST_LEN), (0, 2, 1, 3))
    lists = jnp.where(listed, codes, -1).astype(jnp.int32)
    lists = lists.at[0, full, 0, 0].set(CYCLE_SLOTS * NPHI - 1)
    return (lists.astype(jnp.int32), order[:, :, :LISTED])


def draw_cycle_table(key, part):
    return cycle_layout(key)


def draw_m_values(key, part):
    inner = jax.random.permutation(jax.random.fold_in(key, 3), LMAX - 2)[:M_ALL - 2] + 1
    values = jnp.concatenate([jnp.array([0, LMAX - 1], dtype=jnp.int32), inner.astype(jnp.int32)])
    return jax.random.permutation(jax.random.fold_in(key, 5), values).astype(jnp.int32)


def draw_send_lists(key, part):
    lists, chosen = listing(key)
    return lists


def draw_sample_block(key, part):
    lists, chosen = listing(key)
    picks = jax.random.randint(jax.random.fold_in(key, 23), (NDET, NSAMP), 0, LISTED)
    owners = jnp.arange(NSAMP, dtype=jnp.int32) // S_DEV
    detectors = jnp.arange(NDET, dtype=jnp.int32)
    blocks = chosen[detectors[:, None], owners[None, :], picks]
    blocks = blocks.at[0, 0].set(0)
    blocks = blocks.at[0, 1].set(N_BAND * LIST_LEN - 1)
    return blocks.astype(jnp.int32)


def plant(entries, rng, smallest, top_value):
    longest = entries.shape.index(max(entries.shape))
    spots = []
    for shift in (0, 1):
        where = [jax.random.randint(jax.random.fold_in(rng, axis), (), 0, length) for axis, length in enumerate(entries.shape)]
        where[longest] = (where[longest] + shift) % entries.shape[longest]
        spots.append(tuple(where))
    return entries.at[spots[0]].set(smallest).at[spots[1]].set(top_value)


def shard_levels(stream_key, extent, cuts, least, high):
    gain = 1.0
    for dim, blocks in cuts:
        draws = jax.random.uniform(jax.random.fold_in(jax.random.fold_in(stream_key, 6), dim), (blocks,), jnp.float32, least / len(cuts), high / len(cuts))
        gain = gain * jnp.repeat(jnp.exp(draws), extent[dim] // blocks).reshape((-1,) + (1,) * (len(extent) - 1 - dim))
    return gain


def gaussian(key, shape, deviation, most, shards=(), kind=jnp.bfloat16):
    values = deviation * jax.random.normal(key, shape, jnp.float32)
    if shards:
        values = values * shard_levels(key, shape, shards, -0.22, 0.18)
    return jnp.clip(values, -most, most).astype(kind)


def setup_inputs(seed: int = 0) -> dict:
    arg_keys = jax.random.split(jax.random.key(seed), 11)
    return {
        "sky_coeffs": gaussian(arg_keys[0], (COMP, 2, M_ALL, L), 1.0, 6.0, ((2, 128), (3, 4)), jnp.float32),
        "beam_coeffs": gaussian(arg_keys[1], (NDET, COMP, 2, MPRIME, L), 0.4, 2.5, ((0, 4),)),
        "wigner_panel": gaussian(arg_keys[2], (M_ALL, MPRIME, L, CYCLES), L ** -0.5, 0.125, ((0, 128), (2, 4))),
        "m_values": draw_m_values(jax.random.fold_in(arg_keys[10], 71), 0),
        "cycle_table": draw_cycle_table(jax.random.fold_in(arg_keys[10], 71), 0),
        "send_lists": draw_send_lists(jax.random.fold_in(arg_keys[10], 71), 0),
        "sample_block": draw_sample_block(jax.random.fold_in(arg_keys[10], 71), 0),
        "sample_phi": plant(jax.random.randint(arg_keys[7], (NDET, NSAMP), 0, BLOCK_PHI - 1), jax.random.fold_in(arg_keys[7], 1), 0, (BLOCK_PHI - 1) - 1).astype(jnp.int32),
        "sample_psi": plant(jax.random.randint(arg_keys[8], (NDET, NSAMP), 0, NPSI), jax.random.fold_in(arg_keys[8], 1), 0, NPSI - 1).astype(jnp.int32),
        "sample_frac": jnp.clip(1.0 * jax.random.uniform(arg_keys[9], (2, NDET, NSAMP), jnp.float32) ** shard_levels(arg_keys[9], (2, NDET, NSAMP), ((1, 4), (2, 128)), -0.2, 0.2), 0.0, 1.0),
    }


def psi_apply(coef):
    highest = lax.Precision.HIGHEST
    cells = jnp.arange(NPSI, dtype=jnp.int32)
    orders = jnp.arange(MPRIME, dtype=jnp.int32) - BMAX
    turns = orders[:, None] * cells[None, :] % NPSI
    angle = 2.0 * math.pi / NPSI * turns.astype(jnp.float32)
    cos_psi = jnp.cos(angle)
    sin_psi = jnp.sin(angle)
    real_part = jnp.einsum('mnr,nj->mrj', coef[0], cos_psi, precision=highest) - jnp.einsum('mnr,nj->mrj', coef[1], sin_psi, precision=highest)
    imag_part = jnp.einsum('mnr,nj->mrj', coef[0], sin_psi, precision=highest) + jnp.einsum('mnr,nj->mrj', coef[1], cos_psi, precision=highest)
    return jnp.stack([real_part, imag_part], 0).astype(jnp.bfloat16)

def phi_table(m_values, columns):
    turns = m_values[:, None] * columns[None, :] % NPHI
    angle = 2.0 * math.pi / NPHI * turns.astype(jnp.float32)
    return jnp.concatenate([jnp.cos(angle), -jnp.sin(angle)], 0).astype(jnp.bfloat16)

def reference(sky_coeffs, beam_coeffs, wigner_panel, m_values, cycle_table, send_lists, sample_block, sample_phi, sample_psi, sample_frac):
    highest = lax.Precision.HIGHEST
    beams = beam_coeffs.astype(jnp.float32)
    mix_real = jnp.einsum('cmk,dcnk->dmnk', sky_coeffs[:, 0], beams[:, :, 0], precision=highest) + jnp.einsum('cmk,dcnk->dmnk', sky_coeffs[:, 1], beams[:, :, 1], precision=highest)
    mix_imag = jnp.einsum('cmk,dcnk->dmnk', sky_coeffs[:, 1], beams[:, :, 0], precision=highest) - jnp.einsum('cmk,dcnk->dmnk', sky_coeffs[:, 0], beams[:, :, 1], precision=highest)
    mixed = jnp.stack([mix_real, mix_imag], 1).astype(jnp.bfloat16)
    per_order = jnp.moveaxis(mixed, 2, 0)

    def one_order(pair):
        rows, panel = pair
        return jnp.einsum('dsnk,nkr->dsnr', rows.astype(jnp.float32), panel.astype(jnp.float32), precision=highest)
    coeff = lax.map(one_order, (per_order, wigner_panel))
    scale = 2.0 / math.sqrt(M_ALL * MPRIME)
    table = phi_table(m_values, jnp.arange(NPHI, dtype=jnp.int32)).astype(jnp.float32)
    owners = jnp.arange(NSAMP, dtype=jnp.int32) // S_DEV
    results = []
    for detector in range(NDET):
        upsi = psi_apply(jnp.transpose(coeff[:, detector], (1, 0, 2, 3)))
        rows = jnp.transpose(upsi, (2, 3, 0, 1)).reshape(CYCLES * NPSI, 2 * M_ALL).astype(jnp.float32)
        cube = (jnp.dot(rows, table, precision=highest) * scale).astype(jnp.bfloat16)
        flat_cube = cube.reshape(-1)
        lists = send_lists[detector]
        block = sample_block[detector]
        source = block // LIST_LEN
        entry = block % LIST_LEN
        code = lists[source, owners, entry]
        cycle = cycle_table[source, code // NPHI]
        phi_lo = (code % NPHI + sample_phi[detector]) % NPHI
        phi_hi = (phi_lo + 1) % NPHI
        psi_lo = sample_psi[detector]
        psi_hi = (psi_lo + 1) % NPSI
        low_base = (cycle * NPSI + psi_lo) * NPHI
        high_base = (cycle * NPSI + psi_hi) * NPHI
        value_ll = jnp.take(flat_cube, low_base + phi_lo).astype(jnp.float32)
        value_lh = jnp.take(flat_cube, low_base + phi_hi).astype(jnp.float32)
        value_hl = jnp.take(flat_cube, high_base + phi_lo).astype(jnp.float32)
        value_hh = jnp.take(flat_cube, high_base + phi_hi).astype(jnp.float32)
        frac_p = sample_frac[0, detector]
        frac_q = sample_frac[1, detector]
        low_row = (1.0 - frac_p) * value_ll + frac_p * value_lh
        high_row = (1.0 - frac_p) * value_hl + frac_p * value_hh
        results.append((1.0 - frac_q) * low_row + frac_q * high_row)
    return jnp.stack(results, 0)
```

```python
import functools
import math

import jax
import jax.numpy as jnp
import numpy as np
from jax import lax
from jax.experimental import pallas as pl
from jax.experimental.pallas import tpu as pltpu
from jax.sharding import PartitionSpec as P

BMAX = 8
MPRIME = 17
NPSI = 32
NPHI = 4096
BLOCK_PHI = 128
BANDS = 128
LISTED = 8
ROWS = 4
ORDERS_PAD = 24
CHUNK = 512
UNLISTED = 200.0
MESH = pl.DeviceIdType.MESH


def psi_matrices():
    orders = np.arange(MPRIME) - BMAX
    cells = np.arange(128) % NPSI
    angle = 2.0 * math.pi / NPSI * ((orders[:, None] * cells[None, :]) % NPSI)
    cos_psi, sin_psi = np.cos(angle), np.sin(angle)
    table = np.zeros((2, 2, ORDERS_PAD, 128), np.float32)
    table[0, 0, :MPRIME] = cos_psi
    table[0, 1, :MPRIME] = -sin_psi
    table[1, 0, :MPRIME] = sin_psi
    table[1, 1, :MPRIME] = cos_psi
    return table


def cosine_weights():
    nodes = np.cos(math.pi * (np.arange(64) + 0.5) / 64)
    top = math.pi**2
    squares = (nodes + 1.0) * top / 2
    fit = np.polynomial.chebyshev.Chebyshev.fit(squares, np.cos(np.sqrt(squares)), 8, domain=[0, top])
    weights = fit.convert(kind=np.polynomial.Polynomial).coef
    return [float(w) for w in weights]


COSINE = cosine_weights()


def cosine_of_turns(turns):
    centred = jnp.bitwise_and(turns, NPHI - 1) - NPHI // 2
    angle = centred.astype(jnp.float32) * (2.0 * math.pi / NPHI)
    square = angle * angle
    total = jnp.full_like(square, COSINE[-1])
    for weight in COSINE[-2::-1]:
        total = total * square + weight
    return -total


def iota(shape, axis):
    return lax.broadcasted_iota(jnp.int32, shape, axis)


def dot(a, b):
    return jnp.dot(a, b, preferred_element_type=jnp.float32)


def dot_rows(a, b, precision=None):
    return lax.dot_general(
        a, b, (((0,), (0,)), ((), ())), preferred_element_type=jnp.float32, precision=precision
    )


def ones_where(mask):
    return jnp.where(mask, 1.0, 0.0).astype(jnp.bfloat16)


def list_ranks(codes):
    entries = codes.shape[0]
    listed = codes >= 0
    below = ones_where(iota((entries, entries), 0) > iota((entries, entries), 1))
    rank = dot(below, ones_where(listed))
    return jnp.where(listed, rank, UNLISTED)


def choose_payload(coeff, psi_table, codes, cycles):
    highest = lax.Precision.HIGHEST
    rank = list_ranks(codes)
    both = jnp.concatenate([cycles, cycles], 0)
    slot = lax.shift_right_arithmetic(codes, 12)
    cycle = jnp.where(slot == 0, both[:, 0:1], jnp.where(slot == 1, both[:, 1:2], both[:, 2:3]))
    width = BANDS * ROWS
    spread = ones_where(iota((BANDS, width), 1) // ROWS == iota((BANDS, width), 0))
    rank_wide = dot(rank.astype(jnp.bfloat16), spread)
    cycle_wide = dot(cycle.astype(jnp.float32).astype(jnp.bfloat16), spread)
    place = iota((1, width), 1) % ROWS
    half = place % 2
    lane_group = iota((BANDS, 128), 1) // NPSI
    waves = [
        dot_rows(coeff[0], psi_table[part, 0], highest)
        + dot_rows(coeff[1], psi_table[part, 1], highest)
        for part in range(2)
    ]
    row_cycle = iota((128, width), 0).astype(jnp.float32)
    total = None
    for group in range(4):
        wanted = (4 * half + group).astype(jnp.float32)
        chosen = jnp.sum(jnp.where(rank_wide == wanted, cycle_wide, 0.0), 0, keepdims=True)
        for part in range(2):
            target = jnp.where(place // 2 == part, chosen, -1.0)
            hot = ones_where(row_cycle == target)
            piece = jnp.where(lane_group == group, waves[part], 0.0).astype(jnp.bfloat16)
            term = dot_rows(hot, piece)
            total = term if total is None else total + term
    return total.astype(jnp.bfloat16)


def own_blocks(codes, owner):
    rank = list_ranks(codes)
    entries = codes.shape[0]
    mine = iota((entries, BANDS), 1) == owner
    rank_col = jnp.sum(jnp.where(mine, rank, 0.0), 1, keepdims=True)
    start = jnp.bitwise_and(codes, NPHI - 1).astype(jnp.float32)
    start_col = jnp.sum(jnp.where(mine, start, 0.0), 1, keepdims=True)
    place = iota((entries, 128), 0)
    name = (place % BANDS * 2 + place // BANDS + 1).astype(jnp.float32)
    lanes = iota((entries, 128), 1).astype(jnp.float32)
    picked = rank_col == lanes
    name_row = jnp.sum(jnp.where(picked, name, 0.0), 0, keepdims=True) - 1.0
    start_row = jnp.sum(jnp.where(picked, start_col, 0.0), 0, keepdims=True)
    rows = LISTED * NPSI
    of_row = iota((rows, 128), 0) // NPSI == iota((rows, 128), 1)
    name_col = jnp.sum(jnp.where(of_row, name_row, 0.0), 1, keepdims=True).astype(jnp.int32)
    keys = name_col * NPSI + iota((rows, 1), 0) % NPSI
    rows = LISTED * BLOCK_PHI
    of_row = iota((rows, 128), 0) // BLOCK_PHI == iota((rows, 128), 1)
    first = jnp.sum(jnp.where(of_row, start_row, 0.0), 1, keepdims=True).astype(jnp.int32)
    columns = first + iota((rows, 1), 0) % BLOCK_PHI
    return keys, columns


def block_cells(received, cos_phase, sin_phase, scale):
    width = BANDS * ROWS
    lane_group = iota((BANDS, 128), 1) // NPSI
    halves = []
    for half in range(2):
        total = None
        for part, phase in enumerate((cos_phase, sin_phase)):
            pick = ones_where(
                iota((BANDS, width), 1) == iota((BANDS, width), 0) * ROWS + (2 * part + half)
            )
            rows = dot(pick, received)
            for group in range(4):
                first = (4 * half + group) * BLOCK_PHI
                piece = jnp.where(lane_group == group, rows, 0.0).astype(jnp.bfloat16)
                term = dot(phase[first : first + BLOCK_PHI], piece)
                total = term if total is None else total + term
        halves.append((total * scale).astype(jnp.bfloat16))
    return jnp.concatenate(halves, 1)


def blend(cells, keys, block, cell_phi, cell_psi, frac_phi, frac_psi):
    count = block.shape[1]
    base = block * NPSI
    low = ones_where(keys == base + cell_psi)
    high = ones_where(keys == base + jnp.bitwise_and(cell_psi + 1, NPSI - 1))
    row = (1.0 - frac_psi) * dot(cells, low) + frac_psi * dot(cells, high)
    places = iota((BLOCK_PHI, count), 0)
    weight = jnp.where(places == cell_phi, 1.0 - frac_phi, 0.0)
    weight = jnp.where(places == cell_phi + 1, frac_phi, weight)
    return jnp.sum(weight * row, 0, keepdims=True)


def payload_kernel(coeff_ref, psi_ref, codes_ref, cycles_ref, out_ref):
    out_ref[...] = choose_payload(coeff_ref, psi_ref, codes_ref[...], cycles_ref[...])


def exchange_kernel(bands, src_ref, dst_ref, send_sem, recv_sem, own_sem):
    me = lax.axis_index("band")
    barrier = pltpu.get_barrier_semaphore()

    def greet(step, carry):
        peer = lax.rem(me + step, bands)
        pl.semaphore_signal(barrier, inc=1, device_id={"band": peer}, device_id_type=MESH)
        return carry

    lax.fori_loop(1, bands, greet, 0)
    own = pltpu.make_async_copy(src_ref.at[me], dst_ref.at[me], own_sem)
    own.start()
    pl.semaphore_wait(barrier, bands - 1)

    def send(step, carry):
        peer = lax.rem(me + step, bands)
        pltpu.make_async_remote_copy(
            src_ref=src_ref.at[peer],
            dst_ref=dst_ref.at[me],
            send_sem=send_sem,
            recv_sem=recv_sem,
            device_id={"band": peer},
            device_id_type=MESH,
        ).start()
        return carry

    lax.fori_loop(1, bands, send, 0)
    own.wait()
    others = pl.ds(0, bands - 1)
    everything = pltpu.make_async_remote_copy(
        src_ref=src_ref.at[others],
        dst_ref=dst_ref.at[others],
        send_sem=send_sem,
        recv_sem=recv_sem,
        device_id={"band": me},
        device_id_type=MESH,
    )
    everything.wait_send()
    everything.wait_recv()


def samples_kernel(
    scale,
    owner_ref,
    received_ref,
    codes_ref,
    orders_ref,
    block_ref,
    phi_ref,
    psi_ref,
    frac_ref,
    out_ref,
):
    keys, columns = own_blocks(codes_ref[...], owner_ref[0])
    turns = columns * orders_ref[...]
    cos_phase = cosine_of_turns(turns).astype(jnp.bfloat16)
    sin_phase = cosine_of_turns(turns + NPHI // 4).astype(jnp.bfloat16)
    cells = block_cells(received_ref[...], cos_phase, sin_phase, scale)
    for first in range(0, block_ref.shape[1], CHUNK):
        part = slice(first, first + CHUNK)
        out_ref[:, part] = blend(
            cells,
            keys,
            block_ref[:, part],
            phi_ref[:, part],
            psi_ref[:, part],
            frac_ref[0:1, part],
            frac_ref[1:2, part],
        )


def vmem_specs(count):
    return [pl.BlockSpec(memory_space=pltpu.VMEM)] * count


def per_device(
    sky_coeffs,
    beam_coeffs,
    wigner_panel,
    m_values,
    cycle_table,
    send_lists,
    sample_block,
    sample_phi,
    sample_psi,
    sample_frac,
):
    highest = lax.Precision.HIGHEST
    orders_all = m_values.shape[0]
    scale = 2.0 / math.sqrt(orders_all * MPRIME)
    own_band = lax.axis_index("band")
    beams = lax.all_to_all(beam_coeffs, "det", split_axis=4, concat_axis=0, tiled=True).astype(
        jnp.float32
    )
    mix_real = jnp.einsum(
        "cmk,dcnk->dmnk", sky_coeffs[:, 0], beams[:, :, 0], precision=highest
    ) + jnp.einsum("cmk,dcnk->dmnk", sky_coeffs[:, 1], beams[:, :, 1], precision=highest)
    mix_imag = jnp.einsum(
        "cmk,dcnk->dmnk", sky_coeffs[:, 1], beams[:, :, 0], precision=highest
    ) - jnp.einsum("cmk,dcnk->dmnk", sky_coeffs[:, 0], beams[:, :, 1], precision=highest)
    mixed = jnp.stack([mix_real, mix_imag], 1).astype(jnp.bfloat16)
    coeff = lax.psum_scatter(
        jnp.einsum("dsmnk,mnkr->dsmnr", mixed, wigner_panel, preferred_element_type=jnp.float32),
        "det",
        scatter_dimension=0,
        tiled=True,
    )[0]
    coeff = jnp.pad(coeff[:, 0], ((0, 0), (0, ORDERS_PAD - MPRIME), (0, 0)))
    codes = jnp.transpose(send_lists[0], (2, 0, 1)).reshape(2 * BANDS, BANDS)
    payload = pl.pallas_call(
        payload_kernel,
        out_shape=jax.ShapeDtypeStruct((BANDS * ROWS, 128), jnp.bfloat16),
        in_specs=vmem_specs(4),
        out_specs=vmem_specs(1)[0],
    )(coeff, jnp.asarray(psi_matrices()), codes, cycle_table)
    received = pl.pallas_call(
        functools.partial(exchange_kernel, BANDS),
        out_shape=jax.ShapeDtypeStruct((BANDS, ROWS, 128), jnp.bfloat16),
        in_specs=vmem_specs(1),
        out_specs=vmem_specs(1)[0],
        scratch_shapes=[pltpu.SemaphoreType.DMA] * 3,
        compiler_params=pltpu.CompilerParams(collective_id=0, has_side_effects=True),
    )(payload.reshape(BANDS, ROWS, 128))
    return pl.pallas_call(
        functools.partial(samples_kernel, scale),
        out_shape=jax.ShapeDtypeStruct(sample_block.shape, jnp.float32),
        in_specs=[pl.BlockSpec(memory_space=pltpu.SMEM)] + vmem_specs(7),
        out_specs=vmem_specs(1)[0],
    )(
        own_band.reshape(1),
        received.reshape(BANDS * ROWS, 128),
        codes,
        m_values.reshape(1, orders_all),
        sample_block,
        sample_phi,
        sample_psi,
        sample_frac[:, 0],
    )


def solution(mesh):
    return jax.shard_map(
        per_device,
        mesh=mesh,
        in_specs=(
            P(None, None, "band", "det"),
            P("det", None, None, None, None),
            P("band", None, "det", None),
            P(),
            P(),
            P("det", None, None, None),
            P("det", "band"),
            P("det", "band"),
            P("det", "band"),
            P(None, "det", "band"),
        ),
        out_specs=P("det", "band"),
        check_vma=False,
    )
```

```python
import functools
import math

import jax
import jax.numpy as jnp
import numpy as np
from jax import lax
from jax.experimental import pallas as pl
from jax.experimental.pallas import tpu as pltpu
from jax.sharding import PartitionSpec as P

BMAX = 8
MPRIME = 17
NPSI = 32
NPHI = 4096
BLOCK_PHI = 128
BANDS = 128
LISTED = 8
ROWS = 4
ORDERS_PAD = 40
CHUNK = 512
UNLISTED = 200.0
MESH = pl.DeviceIdType.MESH


def psi_matrices():
    orders = np.arange(MPRIME) - BMAX
    cells = np.arange(128) % NPSI
    angle = 2.0 * math.pi / NPSI * ((orders[:, None] * cells[None, :]) % NPSI)
    cos_psi, sin_psi = np.cos(angle), np.sin(angle)
    table = np.zeros((2, ORDERS_PAD, 128), np.float32)
    table[0, 0 : 2 * MPRIME : 2] = cos_psi
    table[0, 1 : 2 * MPRIME : 2] = -sin_psi
    table[1, 0 : 2 * MPRIME : 2] = sin_psi
    table[1, 1 : 2 * MPRIME : 2] = cos_psi
    return table


def cosine_weights():
    nodes = np.cos(math.pi * (np.arange(64) + 0.5) / 64)
    top = math.pi**2
    squares = (nodes + 1.0) * top / 2
    fit = np.polynomial.chebyshev.Chebyshev.fit(squares, np.cos(np.sqrt(squares)), 8, domain=[0, top])
    weights = fit.convert(kind=np.polynomial.Polynomial).coef
    return [float(w) for w in weights]


COSINE = cosine_weights()


def cosine_of_turns(turns):
    centred = jnp.bitwise_and(turns, NPHI - 1) - NPHI // 2
    angle = centred.astype(jnp.float32) * (2.0 * math.pi / NPHI)
    square = angle * angle
    total = jnp.full_like(square, COSINE[-1])
    for weight in COSINE[-2::-1]:
        total = total * square + weight
    return -total


def iota(shape, axis):
    return lax.broadcasted_iota(jnp.int32, shape, axis)


def dot(a, b):
    return jnp.dot(a, b, preferred_element_type=jnp.float32)


def dot_rows(a, b, precision=None):
    return lax.dot_general(
        a, b, (((0,), (0,)), ((), ())), preferred_element_type=jnp.float32, precision=precision
    )


def ones_where(mask):
    return jnp.where(mask, 1.0, 0.0).astype(jnp.bfloat16)


def list_ranks(codes):
    entries = codes.shape[0]
    listed = codes >= 0
    below = ones_where(iota((entries, entries), 0) > iota((entries, entries), 1))
    rank = dot(below, ones_where(listed))
    return jnp.where(listed, rank, UNLISTED)


def choose_payload(coeff, psi_table, codes, cycles):
    highest = lax.Precision.HIGHEST
    rank = list_ranks(codes)
    entries = codes.shape[0]
    source = ones_where(iota((entries, BANDS), 0) // 2 == iota((entries, BANDS), 1))
    both = lax.dot_general(
        source,
        cycles.astype(jnp.float32).astype(jnp.bfloat16),
        (((1,), (1,)), ((), ())),
        preferred_element_type=jnp.float32,
    )
    slot = lax.shift_right_arithmetic(codes, 12)
    cycle = jnp.where(slot == 0, both[:, 0:1], jnp.where(slot == 1, both[:, 1:2], both[:, 2:3]))
    width = BANDS * ROWS
    spread = ones_where(iota((BANDS, width), 1) // ROWS == iota((BANDS, width), 0))
    rank_wide = dot(rank.astype(jnp.bfloat16), spread)
    cycle_wide = dot(cycle.astype(jnp.bfloat16), spread)
    place = iota((1, width), 1) % ROWS
    half = place % 2
    lane_group = iota((BANDS, 128), 1) // NPSI
    waves = [dot_rows(coeff, psi_table[part], highest) for part in range(2)]
    row_cycle = iota((128, width), 0).astype(jnp.float32)
    total = None
    for group in range(4):
        wanted = (4 * half + group).astype(jnp.float32)
        chosen = jnp.sum(jnp.where(rank_wide == wanted, cycle_wide, 0.0), 0, keepdims=True)
        for part in range(2):
            target = jnp.where(place // 2 == part, chosen, -1.0)
            hot = ones_where(row_cycle == target)
            piece = jnp.where(lane_group == group, waves[part], 0.0).astype(jnp.bfloat16)
            term = dot_rows(hot, piece)
            total = term if total is None else total + term
    return total.astype(jnp.bfloat16)


def own_blocks(codes, owner):
    rank = list_ranks(codes)
    entries = codes.shape[0]
    mine = iota((entries, BANDS), 1) == owner
    rank_col = jnp.sum(jnp.where(mine, rank, 0.0), 1, keepdims=True)
    start = jnp.bitwise_and(codes, NPHI - 1).astype(jnp.float32)
    start_col = jnp.sum(jnp.where(mine, start, 0.0), 1, keepdims=True)
    name = (iota((entries, 128), 0) + 1).astype(jnp.float32)
    lanes = iota((entries, 128), 1).astype(jnp.float32)
    picked = rank_col == lanes
    name_row = jnp.sum(jnp.where(picked, name, 0.0), 0, keepdims=True) - 1.0
    start_row = jnp.sum(jnp.where(picked, start_col, 0.0), 0, keepdims=True)
    rows = LISTED * NPSI
    of_row = iota((rows, 128), 0) // NPSI == iota((rows, 128), 1)
    name_col = jnp.sum(jnp.where(of_row, name_row, 0.0), 1, keepdims=True).astype(jnp.int32)
    keys = name_col * NPSI + iota((rows, 1), 0) % NPSI
    rows = LISTED * BLOCK_PHI
    of_row = iota((rows, 128), 0) // BLOCK_PHI == iota((rows, 128), 1)
    first = jnp.sum(jnp.where(of_row, start_row, 0.0), 1, keepdims=True).astype(jnp.int32)
    columns = first + iota((rows, 1), 0) % BLOCK_PHI
    return keys, columns


def block_cells(received, cos_phase, sin_phase, scale):
    width = BANDS * ROWS
    lane_group = iota((BANDS, 128), 1) // NPSI
    halves = []
    for half in range(2):
        total = None
        for part, phase in enumerate((cos_phase, sin_phase)):
            pick = ones_where(
                iota((BANDS, width), 1) == iota((BANDS, width), 0) * ROWS + (2 * part + half)
            )
            rows = dot(pick, received)
            for group in range(4):
                first = (4 * half + group) * BLOCK_PHI
                piece = jnp.where(lane_group == group, rows, 0.0).astype(jnp.bfloat16)
                term = dot(phase[first : first + BLOCK_PHI], piece)
                total = term if total is None else total + term
        halves.append((total * scale).astype(jnp.bfloat16))
    return jnp.concatenate(halves, 1)


def blend(cells, keys, block, cell_phi, cell_psi, frac_phi, frac_psi):
    count = block.shape[1]
    base = block * NPSI
    low = ones_where(keys == base + cell_psi)
    high = ones_where(keys == base + jnp.bitwise_and(cell_psi + 1, NPSI - 1))
    row = (1.0 - frac_psi) * dot(cells, low) + frac_psi * dot(cells, high)
    places = iota((BLOCK_PHI, count), 0)
    weight = jnp.where(places == cell_phi, 1.0 - frac_phi, 0.0)
    weight = jnp.where(places == cell_phi + 1, frac_phi, weight)
    return jnp.sum(weight * row, 0, keepdims=True)


def coeff_kernel(
    dets,
    beam_ref,
    sky_ref,
    panel_ref,
    out_ref,
    beams,
    panel,
    part,
    parts,
    own_sem,
    send_sem,
    recv_sem,
):
    me = lax.axis_index("det")
    comps, span = beams.shape[1], beams.shape[4]
    rows = 2 * dets
    peers = [lax.rem(me + step, dets) for step in range(dets)]
    barrier = pltpu.get_barrier_semaphore()
    for step in range(1, dets):
        pl.semaphore_signal(
            barrier, inc=1, device_id={"det": peers[step]}, device_id_type=MESH
        )
    own_panel = pltpu.make_async_copy(panel_ref, panel, own_sem.at[0])
    own_panel.start()

    def columns(det):
        return beam_ref.at[:, :, :, pl.ds(pl.multiple_of(det * span, span), span)]

    own_beams = pltpu.make_async_copy(columns(me), beams.at[me], own_sem.at[1])
    own_beams.start()
    pl.semaphore_wait(barrier, dets - 1)

    def remote(stage, step, source, target):
        return pltpu.make_async_remote_copy(
            src_ref=source,
            dst_ref=target,
            send_sem=send_sem.at[stage, step],
            recv_sem=recv_sem.at[stage, step],
            device_id={"det": peers[step]},
            device_id_type=MESH,
        )

    sends = [
        remote(0, step, columns(peers[step]), beams.at[me]) for step in range(1, dets)
    ]
    for copy in sends:
        copy.start()
    own_panel.wait()
    own_beams.wait()
    for copy in sends:
        copy.wait()
    real_row = iota((rows, span), 0) % 2 == 0
    direct, crossed = [], []
    for comp in range(comps):
        first = jnp.broadcast_to(sky_ref[2 * comp], (rows, span))
        direct.append(jnp.where(real_row, first, -first))
        crossed.append(jnp.broadcast_to(sky_ref[2 * comp + 1], (rows, span)))

    def one_order(order, carry):
        mixed = jnp.zeros((rows, span), jnp.float32)
        for comp in range(comps):
            values = jnp.concatenate(
                [beams[det, comp, order].astype(jnp.float32) for det in range(dets)], 0
            )
            swapped = jnp.where(
                real_row, pltpu.roll(values, rows - 1, 0), pltpu.roll(values, 1, 0)
            )
            mixed = mixed + direct[comp] * values + crossed[comp] * swapped
        sums = dot(mixed.astype(jnp.bfloat16), panel[order])
        for det in range(dets):
            part[det, order] = sums[2 * det : 2 * det + 2]
        return carry

    lax.fori_loop(0, MPRIME, one_order, 0)
    sends = [remote(1, step, part.at[peers[step]], parts.at[me]) for step in range(1, dets)]
    for copy in sends:
        copy.start()
    for copy in sends:
        copy.wait()
    out_ref[...] = jnp.zeros_like(out_ref)
    for order in range(MPRIME):
        total = part[me, order]
        for step in range(1, dets):
            total = total + parts[peers[step], order]
        out_ref[2 * order : 2 * order + 2, :] = total


def payload_kernel(coeff_ref, psi_ref, codes_ref, cycles_ref, out_ref):
    out_ref[...] = choose_payload(coeff_ref[...], psi_ref, codes_ref[...], cycles_ref[...])


def exchange_kernel(bands, src_ref, dst_ref, send_sem, recv_sem, own_sem):
    me = lax.axis_index("band")
    barrier = pltpu.get_barrier_semaphore()

    def greet(step, carry):
        peer = lax.rem(me + step, bands)
        pl.semaphore_signal(barrier, inc=1, device_id={"band": peer}, device_id_type=MESH)
        return carry

    lax.fori_loop(1, bands, greet, 0)
    own = pltpu.make_async_copy(src_ref.at[me], dst_ref.at[me], own_sem)
    own.start()
    pl.semaphore_wait(barrier, bands - 1)

    def send(step, carry):
        peer = lax.rem(me + step, bands)
        pltpu.make_async_remote_copy(
            src_ref=src_ref.at[peer],
            dst_ref=dst_ref.at[me],
            send_sem=send_sem,
            recv_sem=recv_sem,
            device_id={"band": peer},
            device_id_type=MESH,
        ).start()
        return carry

    lax.fori_loop(1, bands, send, 0)
    own.wait()
    others = pl.ds(0, bands - 1)
    everything = pltpu.make_async_remote_copy(
        src_ref=src_ref.at[others],
        dst_ref=dst_ref.at[others],
        send_sem=send_sem,
        recv_sem=recv_sem,
        device_id={"band": me},
        device_id_type=MESH,
    )
    everything.wait_send()
    everything.wait_recv()


def samples_kernel(
    scale,
    owner_ref,
    received_ref,
    codes_ref,
    orders_ref,
    block_ref,
    phi_ref,
    psi_ref,
    frac_ref,
    out_ref,
):
    keys, columns = own_blocks(codes_ref[...], owner_ref[0])
    turns = columns * orders_ref[...]
    cos_phase = cosine_of_turns(turns).astype(jnp.bfloat16)
    sin_phase = cosine_of_turns(turns + NPHI // 4).astype(jnp.bfloat16)
    cells = block_cells(received_ref[...], cos_phase, sin_phase, scale)
    for first in range(0, block_ref.shape[1], CHUNK):
        part = slice(first, first + CHUNK)
        out_ref[:, part] = blend(
            cells,
            keys,
            block_ref[:, part],
            phi_ref[:, part],
            psi_ref[:, part],
            frac_ref[0, :, part],
            frac_ref[1, :, part],
        )


def vmem_specs(count):
    return [pl.BlockSpec(memory_space=pltpu.VMEM)] * count


def per_device(
    sky_coeffs,
    beam_coeffs,
    wigner_panel,
    m_values,
    cycle_table,
    send_lists,
    sample_block,
    sample_phi,
    sample_psi,
    sample_frac,
):
    orders_all = m_values.shape[0]
    scale = 2.0 / math.sqrt(orders_all * MPRIME)
    own_band = lax.axis_index("band")
    comps, span = sky_coeffs.shape[0], sky_coeffs.shape[3]
    cycles = wigner_panel.shape[3]
    beams = jnp.transpose(beam_coeffs[0], (0, 2, 1, 3))
    dets = beams.shape[3] // span
    coeff = pl.pallas_call(
        functools.partial(coeff_kernel, dets),
        out_shape=jax.ShapeDtypeStruct((ORDERS_PAD, cycles), jnp.float32),
        in_specs=[
            pl.BlockSpec(memory_space=pl.ANY),
            pl.BlockSpec(memory_space=pltpu.VMEM),
            pl.BlockSpec(memory_space=pl.ANY),
        ],
        out_specs=vmem_specs(1)[0],
        scratch_shapes=[
            pltpu.VMEM((dets, comps, MPRIME, 2, span), jnp.bfloat16),
            pltpu.VMEM((MPRIME, span, cycles), jnp.bfloat16),
            pltpu.VMEM((dets, MPRIME, 2, cycles), jnp.float32),
            pltpu.VMEM((dets, MPRIME, 2, cycles), jnp.float32),
            pltpu.SemaphoreType.DMA((2,)),
            pltpu.SemaphoreType.DMA((2, dets)),
            pltpu.SemaphoreType.DMA((2, dets)),
        ],
        compiler_params=pltpu.CompilerParams(collective_id=1, has_side_effects=True),
    )(beams, sky_coeffs.reshape(2 * comps, 1, span), wigner_panel[0])
    codes = jnp.transpose(send_lists[0], (0, 2, 1)).reshape(2 * BANDS, BANDS)
    payload = pl.pallas_call(
        payload_kernel,
        out_shape=jax.ShapeDtypeStruct((BANDS * ROWS, 128), jnp.bfloat16),
        in_specs=vmem_specs(4),
        out_specs=vmem_specs(1)[0],
    )(coeff, jnp.asarray(psi_matrices()), codes, cycle_table.T)
    received = pl.pallas_call(
        functools.partial(exchange_kernel, BANDS),
        out_shape=jax.ShapeDtypeStruct((BANDS, ROWS, 128), jnp.bfloat16),
        in_specs=vmem_specs(1),
        out_specs=vmem_specs(1)[0],
        scratch_shapes=[pltpu.SemaphoreType.DMA] * 3,
        compiler_params=pltpu.CompilerParams(collective_id=0, has_side_effects=True),
    )(payload.reshape(BANDS, ROWS, 128))
    return pl.pallas_call(
        functools.partial(samples_kernel, scale),
        out_shape=jax.ShapeDtypeStruct(sample_block.shape, jnp.float32),
        in_specs=[pl.BlockSpec(memory_space=pltpu.SMEM)] + vmem_specs(7),
        out_specs=vmem_specs(1)[0],
    )(
        own_band.reshape(1),
        received.reshape(BANDS * ROWS, 128),
        codes,
        m_values.reshape(1, orders_all),
        sample_block,
        sample_phi,
        sample_psi,
        sample_frac,
    )


def solution(mesh):
    return jax.shard_map(
        per_device,
        mesh=mesh,
        in_specs=(
            P(None, None, "band", "det"),
            P("det", None, None, None, None),
            P("band", None, "det", None),
            P(),
            P(),
            P("det", None, None, None),
            P("det", "band"),
            P("det", "band"),
            P("det", "band"),
            P(None, "det", "band"),
        ),
        out_specs=P("det", "band"),
        check_vma=False,
    )
```

```python
import functools
import math

import jax
import jax.numpy as jnp
import numpy as np
from jax import lax
from jax.experimental import pallas as pl
from jax.experimental.pallas import tpu as pltpu
from jax.sharding import PartitionSpec as P

BMAX = 8
MPRIME = 17
NPSI = 32
NPHI = 4096
BLOCK_PHI = 128
BANDS = 128
LISTED = 8
ROWS = 4
ORDERS_PAD = 40
CHUNK = 512
UNLISTED = 200.0
MESH = pl.DeviceIdType.MESH


def psi_matrices():
    orders = np.arange(MPRIME) - BMAX
    cells = np.arange(128) % NPSI
    angle = 2.0 * math.pi / NPSI * ((orders[:, None] * cells[None, :]) % NPSI)
    cos_psi, sin_psi = np.cos(angle), np.sin(angle)
    table = np.zeros((2, ORDERS_PAD, 128), np.float32)
    table[0, 0 : 2 * MPRIME : 2] = cos_psi
    table[0, 1 : 2 * MPRIME : 2] = -sin_psi
    table[1, 0 : 2 * MPRIME : 2] = sin_psi
    table[1, 1 : 2 * MPRIME : 2] = cos_psi
    return table


def cosine_weights():
    nodes = np.cos(math.pi * (np.arange(64) + 0.5) / 64)
    top = math.pi**2
    squares = (nodes + 1.0) * top / 2
    fit = np.polynomial.chebyshev.Chebyshev.fit(squares, np.cos(np.sqrt(squares)), 8, domain=[0, top])
    weights = fit.convert(kind=np.polynomial.Polynomial).coef
    return [float(w) for w in weights]


COSINE = cosine_weights()


def cosine_of_turns(turns):
    centred = jnp.bitwise_and(turns, NPHI - 1) - NPHI // 2
    angle = centred.astype(jnp.float32) * (2.0 * math.pi / NPHI)
    square = angle * angle
    total = jnp.full_like(square, COSINE[-1])
    for weight in COSINE[-2::-1]:
        total = total * square + weight
    return -total


def iota(shape, axis):
    return lax.broadcasted_iota(jnp.int32, shape, axis)


def dot(a, b):
    return jnp.dot(a, b, preferred_element_type=jnp.float32)


def dot_rows(a, b, precision=None):
    return lax.dot_general(
        a, b, (((0,), (0,)), ((), ())), preferred_element_type=jnp.float32, precision=precision
    )


def ones_where(mask):
    return jnp.where(mask, 1.0, 0.0).astype(jnp.bfloat16)


def list_ranks(codes):
    entries = codes.shape[0]
    listed = codes >= 0
    below = ones_where(iota((entries, entries), 0) > iota((entries, entries), 1))
    rank = dot(below, ones_where(listed))
    return jnp.where(listed, rank, UNLISTED)


def payload_places():
    return iota((1, BANDS * ROWS), 1) % ROWS


def choose_cycles(codes, cycles):
    rank = list_ranks(codes)
    entries = codes.shape[0]
    source = ones_where(iota((entries, BANDS), 0) // 2 == iota((entries, BANDS), 1))
    both = lax.dot_general(
        source,
        cycles.astype(jnp.float32).astype(jnp.bfloat16),
        (((1,), (1,)), ((), ())),
        preferred_element_type=jnp.float32,
    )
    slot = lax.shift_right_arithmetic(codes, 12)
    cycle = jnp.where(slot == 0, both[:, 0:1], jnp.where(slot == 1, both[:, 1:2], both[:, 2:3]))
    width = BANDS * ROWS
    spread = ones_where(iota((BANDS, width), 1) // ROWS == iota((BANDS, width), 0))
    rank_wide = dot(rank.astype(jnp.bfloat16), spread)
    cycle_wide = dot(cycle.astype(jnp.bfloat16), spread)
    half = payload_places() % 2
    chosen = []
    for group in range(4):
        wanted = (4 * half + group).astype(jnp.float32)
        chosen.append(
            jnp.sum(jnp.where(rank_wide == wanted, cycle_wide, 0.0), 0, keepdims=True)
        )
    return chosen


def gather_payload(coeff, psi_table, chosen):
    width = BANDS * ROWS
    lane_group = iota((BANDS, 128), 1) // NPSI
    row_cycle = iota((128, width), 0).astype(jnp.float32)
    part_of = payload_places() // 2
    total = None
    for part in range(2):
        waves = dot_rows(coeff, psi_table[part], lax.Precision.HIGHEST)
        for group in range(4):
            target = jnp.where(part_of == part, chosen[group], -1.0)
            hot = ones_where(row_cycle == target)
            piece = jnp.where(lane_group == group, waves, 0.0).astype(jnp.bfloat16)
            term = dot_rows(hot, piece)
            total = term if total is None else total + term
    return total.astype(jnp.bfloat16)


def own_blocks(codes, owner):
    rank = list_ranks(codes)
    entries = codes.shape[0]
    mine = iota((entries, BANDS), 1) == owner
    rank_col = jnp.sum(jnp.where(mine, rank, 0.0), 1, keepdims=True)
    start = jnp.bitwise_and(codes, NPHI - 1).astype(jnp.float32)
    start_col = jnp.sum(jnp.where(mine, start, 0.0), 1, keepdims=True)
    name = (iota((entries, 128), 0) + 1).astype(jnp.float32)
    lanes = iota((entries, 128), 1).astype(jnp.float32)
    picked = rank_col == lanes
    name_row = jnp.sum(jnp.where(picked, name, 0.0), 0, keepdims=True) - 1.0
    start_row = jnp.sum(jnp.where(picked, start_col, 0.0), 0, keepdims=True)
    rows = LISTED * NPSI
    of_row = iota((rows, 128), 0) // NPSI == iota((rows, 128), 1)
    name_col = jnp.sum(jnp.where(of_row, name_row, 0.0), 1, keepdims=True).astype(jnp.int32)
    keys = name_col * NPSI + iota((rows, 1), 0) % NPSI
    rows = LISTED * BLOCK_PHI
    of_row = iota((rows, 128), 0) // BLOCK_PHI == iota((rows, 128), 1)
    first = jnp.sum(jnp.where(of_row, start_row, 0.0), 1, keepdims=True).astype(jnp.int32)
    columns = first + iota((rows, 1), 0) % BLOCK_PHI
    return keys, columns


def block_cells(received, cos_phase, sin_phase, scale):
    width = BANDS * ROWS
    lane_group = iota((BANDS, 128), 1) // NPSI
    halves = []
    for half in range(2):
        total = None
        for part, phase in enumerate((cos_phase, sin_phase)):
            pick = ones_where(
                iota((BANDS, width), 1) == iota((BANDS, width), 0) * ROWS + (2 * part + half)
            )
            rows = dot(pick, received)
            for group in range(4):
                first = (4 * half + group) * BLOCK_PHI
                piece = jnp.where(lane_group == group, rows, 0.0).astype(jnp.bfloat16)
                term = dot(phase[first : first + BLOCK_PHI], piece)
                total = term if total is None else total + term
        halves.append((total * scale).astype(jnp.bfloat16))
    return jnp.concatenate(halves, 1)


def blend(cells, keys, block, cell_phi, cell_psi, frac_phi, frac_psi):
    count = block.shape[1]
    base = block * NPSI
    low = ones_where(keys == base + cell_psi)
    high = ones_where(keys == base + jnp.bitwise_and(cell_psi + 1, NPSI - 1))
    row = (1.0 - frac_psi) * dot(cells, low) + frac_psi * dot(cells, high)
    places = iota((BLOCK_PHI, count), 0)
    weight = jnp.where(places == cell_phi, 1.0 - frac_phi, 0.0)
    weight = jnp.where(places == cell_phi + 1, frac_phi, weight)
    return jnp.sum(weight * row, 0, keepdims=True)


def signal_kernel(
    bands,
    dets,
    scale,
    beam_ref,
    panel_ref,
    sky_in,
    psi_in,
    codes_in,
    cycles_in,
    orders_in,
    block_in,
    phi_in,
    cell_in,
    frac_in,
    out_ref,
    beams,
    panel,
    part,
    parts,
    coeff,
    chosen_ref,
    keys_ref,
    cos_ref,
    sin_ref,
    payload,
    received,
    sky_ref,
    psi_ref,
    codes_ref,
    cycles_ref,
    orders_ref,
    block_ref,
    phi_ref,
    cell_ref,
    frac_ref,
    in_sem,
    own_sem,
    send_sem,
    recv_sem,
    out_sem,
    all_sem,
):
    me = lax.axis_index("det")
    owner = lax.axis_index("band")
    comps, span = beams.shape[1], beams.shape[4]
    rows = 2 * dets
    peers = [lax.rem(me + step, dets) for step in range(dets)]
    barrier = pltpu.get_barrier_semaphore()

    def greet(step, carry):
        peer = lax.rem(owner + step, bands)
        pl.semaphore_signal(barrier, inc=1, device_id={"band": peer}, device_id_type=MESH)
        return carry

    lax.fori_loop(1, bands, greet, 0)
    for step in range(1, dets):
        pl.semaphore_signal(
            barrier, inc=1, device_id={"det": peers[step]}, device_id_type=MESH
        )
    staged = [
        (codes_in, codes_ref),
        (cycles_in, cycles_ref),
        (orders_in, orders_ref),
        (sky_in, sky_ref),
        (psi_in, psi_ref),
        (block_in, block_ref),
        (phi_in, phi_ref),
        (cell_in, cell_ref),
        (frac_in, frac_ref),
    ]
    loads = [
        pltpu.make_async_copy(source, target, in_sem.at[place])
        for place, (source, target) in enumerate(staged)
    ]
    for load in loads:
        load.start()
    own_panel = pltpu.make_async_copy(panel_ref, panel, own_sem.at[0])
    own_panel.start()

    def columns(det):
        return beam_ref.at[:, :, :, pl.ds(pl.multiple_of(det * span, span), span)]

    own_beams = pltpu.make_async_copy(columns(me), beams.at[me], own_sem.at[1])
    own_beams.start()
    for load in loads:
        load.wait()
    for group, row in enumerate(choose_cycles(codes_ref[...], cycles_ref[...])):
        chosen_ref[group : group + 1, :] = row
    keys, places = own_blocks(codes_ref[...], owner)
    keys_ref[...] = jnp.broadcast_to(keys, keys_ref.shape)
    pl.semaphore_wait(barrier, bands - 1 + dets - 1)

    def remote(stage, step, source, target):
        return pltpu.make_async_remote_copy(
            src_ref=source,
            dst_ref=target,
            send_sem=send_sem.at[stage, step],
            recv_sem=recv_sem.at[stage, step],
            device_id={"det": peers[step]},
            device_id_type=MESH,
        )

    sends = [
        remote(0, step, columns(peers[step]), beams.at[me]) for step in range(1, dets)
    ]
    for copy in sends:
        copy.start()
    turns = places * orders_ref[...]
    cos_ref[...] = cosine_of_turns(turns).astype(jnp.bfloat16)
    sin_ref[...] = cosine_of_turns(turns + NPHI // 4).astype(jnp.bfloat16)
    own_panel.wait()
    own_beams.wait()
    for copy in sends:
        copy.wait()
    real_row = iota((rows, span), 0) % 2 == 0
    direct, crossed = [], []
    for comp in range(comps):
        first = jnp.broadcast_to(sky_ref[2 * comp], (rows, span))
        direct.append(jnp.where(real_row, first, -first))
        crossed.append(jnp.broadcast_to(sky_ref[2 * comp + 1], (rows, span)))

    def one_order(order, carry):
        mixed = jnp.zeros((rows, span), jnp.float32)
        for comp in range(comps):
            values = jnp.concatenate(
                [beams[det, comp, order].astype(jnp.float32) for det in range(dets)], 0
            )
            swapped = jnp.where(
                real_row, pltpu.roll(values, rows - 1, 0), pltpu.roll(values, 1, 0)
            )
            mixed = mixed + direct[comp] * values + crossed[comp] * swapped
        sums = dot(mixed.astype(jnp.bfloat16), panel[order])
        for det in range(dets):
            part[det, order] = sums[2 * det : 2 * det + 2]
        return carry

    lax.fori_loop(0, MPRIME, one_order, 0)
    sends = [remote(1, step, part.at[peers[step]], parts.at[me]) for step in range(1, dets)]
    for copy in sends:
        copy.start()
    for copy in sends:
        copy.wait()
    coeff[...] = jnp.zeros_like(coeff)
    for order in range(MPRIME):
        total = part[me, order]
        for step in range(1, dets):
            total = total + parts[peers[step], order]
        coeff[2 * order : 2 * order + 2, :] = total
    chosen = [chosen_ref[group : group + 1, :] for group in range(4)]
    payload[...] = gather_payload(coeff[...], psi_ref, chosen).reshape(payload.shape)
    own = pltpu.make_async_copy(payload.at[owner], received.at[owner], own_sem.at[2])
    own.start()

    def send(step, carry):
        peer = lax.rem(owner + step, bands)
        pltpu.make_async_remote_copy(
            src_ref=payload.at[peer],
            dst_ref=received.at[owner],
            send_sem=out_sem,
            recv_sem=all_sem,
            device_id={"band": peer},
            device_id_type=MESH,
        ).start()
        return carry

    lax.fori_loop(1, bands, send, 0)
    own.wait()
    others = pl.ds(0, bands - 1)
    everything = pltpu.make_async_remote_copy(
        src_ref=payload.at[others],
        dst_ref=received.at[others],
        send_sem=out_sem,
        recv_sem=all_sem,
        device_id={"band": owner},
        device_id_type=MESH,
    )
    everything.wait_recv()
    cells = block_cells(
        received[...].reshape(BANDS * ROWS, 128), cos_ref, sin_ref, scale
    )
    keys = keys_ref[:, 0:1]
    for first in range(0, block_ref.shape[1], CHUNK):
        piece = slice(first, first + CHUNK)
        out_ref[:, piece] = blend(
            cells,
            keys,
            block_ref[:, piece],
            phi_ref[:, piece],
            cell_ref[:, piece],
            frac_ref[0, :, piece],
            frac_ref[1, :, piece],
        )
    everything.wait_send()


def per_device(
    sky_coeffs,
    beam_coeffs,
    wigner_panel,
    m_values,
    cycle_table,
    send_lists,
    sample_block,
    sample_phi,
    sample_psi,
    sample_frac,
):
    orders_all = m_values.shape[0]
    scale = 2.0 / math.sqrt(orders_all * MPRIME)
    comps, span = sky_coeffs.shape[0], sky_coeffs.shape[3]
    cycles = wigner_panel.shape[3]
    beams = jnp.transpose(beam_coeffs[0], (0, 2, 1, 3))
    dets = beams.shape[3] // span
    samples = sample_block.shape[1]
    codes = jnp.transpose(send_lists[0], (0, 2, 1)).reshape(2 * BANDS, BANDS)
    small = [
        sky_coeffs.reshape(2 * comps, 1, span),
        jnp.asarray(psi_matrices()),
        codes,
        cycle_table.T,
        m_values.reshape(1, orders_all),
        sample_block,
        sample_phi,
        sample_psi,
        sample_frac,
    ]
    return pl.pallas_call(
        functools.partial(signal_kernel, BANDS, dets, scale),
        out_shape=jax.ShapeDtypeStruct((1, samples), jnp.float32),
        in_specs=[pl.BlockSpec(memory_space=pl.ANY)] * (2 + len(small)),
        out_specs=pl.BlockSpec(memory_space=pltpu.VMEM),
        scratch_shapes=[
            pltpu.VMEM((dets, comps, MPRIME, 2, span), jnp.bfloat16),
            pltpu.VMEM((MPRIME, span, cycles), jnp.bfloat16),
            pltpu.VMEM((dets, MPRIME, 2, cycles), jnp.float32),
            pltpu.VMEM((dets, MPRIME, 2, cycles), jnp.float32),
            pltpu.VMEM((ORDERS_PAD, cycles), jnp.float32),
            pltpu.VMEM((4, BANDS * ROWS), jnp.float32),
            pltpu.VMEM((LISTED * NPSI, 128), jnp.int32),
            pltpu.VMEM((LISTED * BLOCK_PHI, orders_all), jnp.bfloat16),
            pltpu.VMEM((LISTED * BLOCK_PHI, orders_all), jnp.bfloat16),
            pltpu.VMEM((BANDS, ROWS, 128), jnp.bfloat16),
            pltpu.VMEM((BANDS, ROWS, 128), jnp.bfloat16),
        ]
        + [pltpu.VMEM(array.shape, array.dtype) for array in small]
        + [
            pltpu.SemaphoreType.DMA((len(small),)),
            pltpu.SemaphoreType.DMA((3,)),
            pltpu.SemaphoreType.DMA((2, dets)),
            pltpu.SemaphoreType.DMA((2, dets)),
            pltpu.SemaphoreType.DMA,
            pltpu.SemaphoreType.DMA,
        ],
        compiler_params=pltpu.CompilerParams(collective_id=0, has_side_effects=True),
    )(beams, wigner_panel[0], *small)


def solution(mesh):
    return jax.shard_map(
        per_device,
        mesh=mesh,
        in_specs=(
            P(None, None, "band", "det"),
            P("det", None, None, None, None),
            P("band", None, "det", None),
            P(),
            P(),
            P("det", None, None, None),
            P("det", "band"),
            P("det", "band"),
            P("det", "band"),
            P(None, "det", "band"),
        ),
        out_specs=P("det", "band"),
        check_vma=False,
    )
```

```python
import functools
import math

import jax
import jax.numpy as jnp
import numpy as np
from jax import lax
from jax.experimental import pallas as pl
from jax.experimental.pallas import tpu as pltpu
from jax.sharding import PartitionSpec as P

BMAX = 8
MPRIME = 17
NPSI = 32
NPHI = 4096
BLOCK_PHI = 128
BANDS = 128
LISTED = 8
ROWS = 4
ORDERS_PAD = 40
CHUNK = 512
LINE = 16
ORDER_CUTS = (0, 6, 12, 17)
UNLISTED = 200.0
MESH = pl.DeviceIdType.MESH


def psi_matrices():
    orders = np.arange(MPRIME) - BMAX
    cells = np.arange(128) % NPSI
    angle = 2.0 * math.pi / NPSI * ((orders[:, None] * cells[None, :]) % NPSI)
    cos_psi, sin_psi = np.cos(angle), np.sin(angle)
    table = np.zeros((2, ORDERS_PAD, 128), np.float32)
    table[0, 0 : 2 * MPRIME : 2] = cos_psi
    table[0, 1 : 2 * MPRIME : 2] = -sin_psi
    table[1, 0 : 2 * MPRIME : 2] = sin_psi
    table[1, 1 : 2 * MPRIME : 2] = cos_psi
    return table


def cosine_weights():
    nodes = np.cos(math.pi * (np.arange(64) + 0.5) / 64)
    top = math.pi**2
    squares = (nodes + 1.0) * top / 2
    fit = np.polynomial.chebyshev.Chebyshev.fit(squares, np.cos(np.sqrt(squares)), 8, domain=[0, top])
    weights = fit.convert(kind=np.polynomial.Polynomial).coef
    return [float(w) for w in weights]


COSINE = cosine_weights()


def cosine_of_turns(turns):
    centred = jnp.bitwise_and(turns, NPHI - 1) - NPHI // 2
    angle = centred.astype(jnp.float32) * (2.0 * math.pi / NPHI)
    square = angle * angle
    total = jnp.full_like(square, COSINE[-1])
    for weight in COSINE[-2::-1]:
        total = total * square + weight
    return -total


def iota(shape, axis):
    return lax.broadcasted_iota(jnp.int32, shape, axis)


def dot(a, b):
    return jnp.dot(a, b, preferred_element_type=jnp.float32)


def dot_rows(a, b, precision=None):
    return lax.dot_general(
        a, b, (((0,), (0,)), ((), ())), preferred_element_type=jnp.float32, precision=precision
    )


def ones_where(mask):
    return jnp.where(mask, 1.0, 0.0).astype(jnp.bfloat16)


def list_ranks(codes):
    entries = codes.shape[0]
    listed = codes >= 0
    below = ones_where(iota((entries, entries), 0) > iota((entries, entries), 1))
    rank = dot(below, ones_where(listed))
    return jnp.where(listed, rank, UNLISTED)


def payload_places():
    return iota((1, BANDS * ROWS), 1) % ROWS


def choose_cycles(codes, cycles):
    rank = list_ranks(codes)
    entries = codes.shape[0]
    source = ones_where(iota((entries, BANDS), 0) // 2 == iota((entries, BANDS), 1))
    both = lax.dot_general(
        source,
        cycles.astype(jnp.float32).astype(jnp.bfloat16),
        (((1,), (1,)), ((), ())),
        preferred_element_type=jnp.float32,
    )
    slot = lax.shift_right_arithmetic(codes, 12)
    cycle = jnp.where(slot == 0, both[:, 0:1], jnp.where(slot == 1, both[:, 1:2], both[:, 2:3]))
    width = BANDS * ROWS
    spread = ones_where(iota((BANDS, width), 1) // ROWS == iota((BANDS, width), 0))
    rank_wide = dot(rank.astype(jnp.bfloat16), spread)
    cycle_wide = dot(cycle.astype(jnp.bfloat16), spread)
    half = payload_places() % 2
    chosen = []
    for group in range(4):
        wanted = (4 * half + group).astype(jnp.float32)
        chosen.append(
            jnp.sum(jnp.where(rank_wide == wanted, cycle_wide, 0.0), 0, keepdims=True)
        )
    return chosen


def payload_masks(chosen):
    width = BANDS * ROWS
    part_of = payload_places() // 2
    rows = [
        jnp.where(part_of == part, chosen[group], -1.0) for part in range(2) for group in range(4)
    ]
    targets = jnp.transpose(jnp.concatenate(rows, 0))
    cycle = iota((width, 128), 1).astype(jnp.float32)
    return [ones_where(cycle == targets[:, place : place + 1]) for place in range(len(rows))]


def payload_waves(coeff, psi_table):
    lane_group = iota((BANDS, 128), 1) // NPSI
    pieces = []
    for part in range(2):
        waves = dot_rows(coeff, psi_table[part], lax.Precision.HIGHEST)
        for group in range(4):
            pieces.append(jnp.where(lane_group == group, waves, 0.0).astype(jnp.bfloat16))
    return jnp.concatenate(pieces, 0)


def own_blocks(codes, owner):
    rank = list_ranks(codes)
    entries = codes.shape[0]
    mine = iota((entries, BANDS), 1) == owner
    rank_col = jnp.sum(jnp.where(mine, rank, 0.0), 1, keepdims=True)
    start = jnp.bitwise_and(codes, NPHI - 1).astype(jnp.float32)
    start_col = jnp.sum(jnp.where(mine, start, 0.0), 1, keepdims=True)
    name = (iota((entries, 128), 0) + 1).astype(jnp.float32)
    lanes = iota((entries, 128), 1).astype(jnp.float32)
    picked = rank_col == lanes
    name_row = jnp.sum(jnp.where(picked, name, 0.0), 0, keepdims=True) - 1.0
    start_row = jnp.sum(jnp.where(picked, start_col, 0.0), 0, keepdims=True)
    rows = LISTED * NPSI
    of_row = iota((rows, 128), 0) // NPSI == iota((rows, 128), 1)
    name_col = jnp.sum(jnp.where(of_row, name_row, 0.0), 1, keepdims=True).astype(jnp.int32)
    keys = name_col * NPSI + iota((rows, 1), 0) % NPSI
    rows = LISTED * BLOCK_PHI
    of_row = iota((rows, 128), 0) // BLOCK_PHI == iota((rows, 128), 1)
    first = jnp.sum(jnp.where(of_row, start_row, 0.0), 1, keepdims=True).astype(jnp.int32)
    columns = first + iota((rows, 1), 0) % BLOCK_PHI
    return keys, columns


def block_cells(received, cos_phase, sin_phase, scale):
    width = BANDS * ROWS
    lane_group = iota((BANDS, 128), 1) // NPSI
    halves = []
    for half in range(2):
        total = None
        for part, phase in enumerate((cos_phase, sin_phase)):
            pick = ones_where(
                iota((BANDS, width), 1) == iota((BANDS, width), 0) * ROWS + (2 * part + half)
            )
            rows = dot(pick, received)
            for group in range(4):
                first = (4 * half + group) * BLOCK_PHI
                piece = jnp.where(lane_group == group, rows, 0.0).astype(jnp.bfloat16)
                term = dot(phase[first : first + BLOCK_PHI], piece)
                total = term if total is None else total + term
        halves.append((total * scale).astype(jnp.bfloat16))
    return jnp.concatenate(halves, 1)


def blend_masks(keys, block, cell_psi):
    base = block * NPSI
    low = ones_where(keys == base + cell_psi)
    high = ones_where(keys == base + jnp.bitwise_and(cell_psi + 1, NPSI - 1))
    return low, high


def blend_weights(cell_phi, frac_phi, frac_psi):
    places = iota((BLOCK_PHI, cell_phi.shape[1]), 0)
    weight = jnp.where(places == cell_phi, 1.0 - frac_phi, 0.0)
    weight = jnp.where(places == cell_phi + 1, frac_phi, weight)
    return weight * (1.0 - frac_psi), weight * frac_psi


def signal_kernel(
    bands,
    dets,
    scale,
    beam_ref,
    panel_ref,
    sky_in,
    psi_in,
    codes_in,
    cycles_in,
    orders_in,
    block_in,
    phi_in,
    cell_in,
    frac_in,
    out_ref,
    beams,
    panel,
    part,
    parts,
    coeff,
    hot_ref,
    low_ref,
    high_ref,
    low_weight,
    high_weight,
    keys_ref,
    cos_ref,
    sin_ref,
    payload,
    received,
    sky_ref,
    psi_ref,
    codes_ref,
    cycles_ref,
    orders_ref,
    block_ref,
    phi_ref,
    cell_ref,
    frac_ref,
    in_sem,
    own_sem,
    send_sem,
    recv_sem,
    out_sem,
    all_sem,
):
    me = lax.axis_index("det")
    owner = lax.axis_index("band")
    comps, span = beams.shape[1], beams.shape[4]
    rows = 2 * dets
    peers = [lax.rem(me + step, dets) for step in range(dets)]
    barrier = pltpu.get_barrier_semaphore()

    def far_first(act):
        around = LINE // 2
        shifts = [
            around + (turn // 2 if turn % 2 == 0 else -(turn + 1) // 2)
            for turn in range(bands // LINE)
        ]
        line = lax.rem(owner, LINE)
        column = owner // LINE
        for shift in [bands // (2 * LINE) + value - around for value in shifts]:
            first = lax.rem(column + shift, bands // LINE) * LINE

            def one(step, carry):
                act(first + lax.rem(line + step, LINE))
                return carry

            if shift == 0:
                lax.fori_loop(1, LINE, one, 0)
            else:
                lax.fori_loop(around, around + LINE, one, 0, unroll=4)

    def greet(peer):
        pl.semaphore_signal(barrier, inc=1, device_id={"band": peer}, device_id_type=MESH)

    far_first(greet)
    for step in range(1, dets):
        pl.semaphore_signal(
            barrier, inc=1, device_id={"det": peers[step]}, device_id_type=MESH
        )
    staged = [
        (codes_in, codes_ref),
        (cycles_in, cycles_ref),
        (orders_in, orders_ref),
        (sky_in, sky_ref),
        (psi_in, psi_ref),
        (block_in, block_ref),
        (phi_in, phi_ref),
        (cell_in, cell_ref),
        (frac_in, frac_ref),
    ]
    loads = [
        pltpu.make_async_copy(source, target, in_sem.at[place])
        for place, (source, target) in enumerate(staged)
    ]
    for load in loads:
        load.start()
    own_panel = pltpu.make_async_copy(panel_ref, panel, own_sem.at[0])
    own_panel.start()

    def columns(det, orders):
        return beam_ref.at[:, orders, :, pl.ds(pl.multiple_of(det * span, span), span)]

    every_order = pl.ds(0, MPRIME)
    own_beams = pltpu.make_async_copy(columns(me, every_order), beams.at[me], own_sem.at[1])
    own_beams.start()
    for load in loads:
        load.wait()
    chosen = choose_cycles(codes_ref[...], cycles_ref[...])
    for place, hot in enumerate(payload_masks(chosen)):
        hot_ref[:, place * 128 : place * 128 + 128] = hot
    keys, places = own_blocks(codes_ref[...], owner)
    keys_ref[...] = jnp.broadcast_to(keys, keys_ref.shape)
    pl.semaphore_wait(barrier, bands - 1 + dets - 1)

    def remote(stage, step, source, target):
        return pltpu.make_async_remote_copy(
            src_ref=source,
            dst_ref=target,
            send_sem=send_sem.at[stage, step],
            recv_sem=recv_sem.at[stage, step],
            device_id={"det": peers[step]},
            device_id_type=MESH,
        )

    cuts = [
        pl.ds(first, last - first) for first, last in zip(ORDER_CUTS[:-1], ORDER_CUTS[1:])
    ]
    beam_sends = [
        [
            remote(
                stage, step, columns(peers[step], orders), beams.at[me, :, orders]
            )
            for step in range(1, dets)
        ]
        for stage, orders in enumerate(cuts)
    ]
    for copy in [copy for stage in beam_sends for copy in stage]:
        copy.start()
    turns = places * orders_ref[...]
    cos_ref[...] = cosine_of_turns(turns).astype(jnp.bfloat16)
    sin_ref[...] = cosine_of_turns(turns + NPHI // 4).astype(jnp.bfloat16)
    own_panel.wait()
    own_beams.wait()
    real_row = iota((rows, span), 0) % 2 == 0
    direct, crossed = [], []
    for comp in range(comps):
        first = jnp.broadcast_to(sky_ref[2 * comp], (rows, span))
        direct.append(jnp.where(real_row, first, -first))
        crossed.append(jnp.broadcast_to(sky_ref[2 * comp + 1], (rows, span)))

    def one_order(order, carry):
        mixed = jnp.zeros((rows, span), jnp.float32)
        for comp in range(comps):
            values = jnp.concatenate(
                [beams[det, comp, order].astype(jnp.float32) for det in range(dets)], 0
            )
            swapped = jnp.where(
                real_row, pltpu.roll(values, rows - 1, 0), pltpu.roll(values, 1, 0)
            )
            mixed = mixed + direct[comp] * values + crossed[comp] * swapped
        sums = dot(mixed.astype(jnp.bfloat16), panel[order])
        for det in range(dets):
            part[det, order] = sums[2 * det : 2 * det + 2]
        return carry

    sums_sends = []
    for stage, orders in enumerate(cuts):
        for copy in beam_sends[stage]:
            copy.wait()
        lax.fori_loop(ORDER_CUTS[stage], ORDER_CUTS[stage + 1], one_order, 0)
        for step in range(1, dets):
            copy = remote(
                len(cuts) + stage, step, part.at[peers[step], orders], parts.at[me, orders]
            )
            copy.start()
            sums_sends.append(copy)
    for copy in sums_sends:
        copy.wait()
    coeff[...] = jnp.zeros_like(coeff)
    for order in range(MPRIME):
        total = part[me, order]
        for step in range(1, dets):
            total = total + parts[peers[step], order]
        coeff[2 * order : 2 * order + 2, :] = total
    picked = dot(hot_ref[...], payload_waves(coeff[...], psi_ref))
    payload[...] = picked.astype(jnp.bfloat16).reshape(payload.shape)
    own = pltpu.make_async_copy(payload.at[owner], received.at[owner], own_sem.at[2])
    own.start()

    def send(peer):
        pltpu.make_async_remote_copy(
            src_ref=payload.at[peer],
            dst_ref=received.at[owner],
            send_sem=out_sem,
            recv_sem=all_sem,
            device_id={"band": peer},
            device_id_type=MESH,
        ).start()

    far_first(send)
    keys = keys_ref[:, 0:1]
    pieces = [
        slice(first, first + CHUNK) for first in range(0, block_ref.shape[1], CHUNK)
    ]
    for piece in pieces:
        low, high = blend_masks(keys, block_ref[:, piece], cell_ref[:, piece])
        low_ref[:, piece] = low
        high_ref[:, piece] = high
        low_part, high_part = blend_weights(
            phi_ref[:, piece], frac_ref[0, :, piece], frac_ref[1, :, piece]
        )
        low_weight[:, piece] = low_part
        high_weight[:, piece] = high_part
    own.wait()
    others = pl.ds(0, bands - 1)
    everything = pltpu.make_async_remote_copy(
        src_ref=payload.at[others],
        dst_ref=received.at[others],
        send_sem=out_sem,
        recv_sem=all_sem,
        device_id={"band": owner},
        device_id_type=MESH,
    )
    everything.wait_recv()
    cells = block_cells(
        received[...].reshape(BANDS * ROWS, 128), cos_ref, sin_ref, scale
    )
    for piece in pieces:
        value = low_weight[:, piece] * dot(cells, low_ref[:, piece])
        value = value + high_weight[:, piece] * dot(cells, high_ref[:, piece])
        out_ref[:, piece] = jnp.sum(value, 0, keepdims=True)
    everything.wait_send()


def per_device(
    sky_coeffs,
    beam_coeffs,
    wigner_panel,
    m_values,
    cycle_table,
    send_lists,
    sample_block,
    sample_phi,
    sample_psi,
    sample_frac,
):
    orders_all = m_values.shape[0]
    scale = 2.0 / math.sqrt(orders_all * MPRIME)
    comps, span = sky_coeffs.shape[0], sky_coeffs.shape[3]
    cycles = wigner_panel.shape[3]
    beams = jnp.transpose(beam_coeffs[0], (0, 2, 1, 3))
    dets = beams.shape[3] // span
    samples = sample_block.shape[1]
    codes = jnp.transpose(send_lists[0], (0, 2, 1)).reshape(2 * BANDS, BANDS)
    small = [
        sky_coeffs.reshape(2 * comps, 1, span),
        jnp.asarray(psi_matrices()),
        codes,
        cycle_table.T,
        m_values.reshape(1, orders_all),
        sample_block,
        sample_phi,
        sample_psi,
        sample_frac,
    ]
    return pl.pallas_call(
        functools.partial(signal_kernel, BANDS, dets, scale),
        out_shape=jax.ShapeDtypeStruct((1, samples), jnp.float32),
        in_specs=[pl.BlockSpec(memory_space=pl.ANY)] * (2 + len(small)),
        out_specs=pl.BlockSpec(memory_space=pltpu.VMEM),
        scratch_shapes=[
            pltpu.VMEM((dets, comps, MPRIME, 2, span), jnp.bfloat16),
            pltpu.VMEM((MPRIME, span, cycles), jnp.bfloat16),
            pltpu.VMEM((dets, MPRIME, 2, cycles), jnp.float32),
            pltpu.VMEM((dets, MPRIME, 2, cycles), jnp.float32),
            pltpu.VMEM((ORDERS_PAD, cycles), jnp.float32),
            pltpu.VMEM((BANDS * ROWS, 8 * cycles), jnp.bfloat16),
            pltpu.VMEM((LISTED * NPSI, samples), jnp.bfloat16),
            pltpu.VMEM((LISTED * NPSI, samples), jnp.bfloat16),
            pltpu.VMEM((BLOCK_PHI, samples), jnp.float32),
            pltpu.VMEM((BLOCK_PHI, samples), jnp.float32),
            pltpu.VMEM((LISTED * NPSI, 128), jnp.int32),
            pltpu.VMEM((LISTED * BLOCK_PHI, orders_all), jnp.bfloat16),
            pltpu.VMEM((LISTED * BLOCK_PHI, orders_all), jnp.bfloat16),
            pltpu.VMEM((BANDS, ROWS, 128), jnp.bfloat16),
            pltpu.VMEM((BANDS, ROWS, 128), jnp.bfloat16),
        ]
        + [pltpu.VMEM(array.shape, array.dtype) for array in small]
        + [
            pltpu.SemaphoreType.DMA((len(small),)),
            pltpu.SemaphoreType.DMA((3,)),
            pltpu.SemaphoreType.DMA((2 * len(ORDER_CUTS) - 2, dets)),
            pltpu.SemaphoreType.DMA((2 * len(ORDER_CUTS) - 2, dets)),
            pltpu.SemaphoreType.DMA,
            pltpu.SemaphoreType.DMA,
        ],
        compiler_params=pltpu.CompilerParams(collective_id=0, has_side_effects=True),
    )(beams, wigner_panel[0], *small)


def solution(mesh):
    return jax.shard_map(
        per_device,
        mesh=mesh,
        in_specs=(
            P(None, None, "band", "det"),
            P("det", None, None, None, None),
            P("band", None, "det", None),
            P(),
            P(),
            P("det", None, None, None),
            P("det", "band"),
            P("det", "band"),
            P("det", "band"),
            P(None, "det", "band"),
        ),
        out_specs=P("det", "band"),
        check_vma=False,
    )
```

```python
import functools
import math

import jax
import jax.numpy as jnp
import numpy as np
from jax import lax
from jax.experimental import pallas as pl
from jax.experimental.pallas import tpu as pltpu
from jax.sharding import PartitionSpec as P

BMAX = 8
MPRIME = 17
NPSI = 32
NPHI = 4096
BLOCK_PHI = 128
BANDS = 128
LISTED = 8
ROWS = 4
ORDERS_PAD = 40
CHUNK = 512
LINE = 16
ORDER_CUTS = (0, 5, 10, 14, 17)
UNLISTED = 200.0
MESH = pl.DeviceIdType.MESH


def psi_matrices():
    orders = np.arange(MPRIME) - BMAX
    cells = np.arange(128) % NPSI
    angle = 2.0 * math.pi / NPSI * ((orders[:, None] * cells[None, :]) % NPSI)
    cos_psi, sin_psi = np.cos(angle), np.sin(angle)
    table = np.zeros((2, ORDERS_PAD, 128), np.float32)
    table[0, 0 : 2 * MPRIME : 2] = cos_psi
    table[0, 1 : 2 * MPRIME : 2] = -sin_psi
    table[1, 0 : 2 * MPRIME : 2] = sin_psi
    table[1, 1 : 2 * MPRIME : 2] = cos_psi
    return table


def cosine_weights():
    nodes = np.cos(math.pi * (np.arange(64) + 0.5) / 64)
    top = math.pi**2
    squares = (nodes + 1.0) * top / 2
    fit = np.polynomial.chebyshev.Chebyshev.fit(squares, np.cos(np.sqrt(squares)), 8, domain=[0, top])
    weights = fit.convert(kind=np.polynomial.Polynomial).coef
    return [float(w) for w in weights]


COSINE = cosine_weights()


def cosine_of_turns(turns):
    centred = jnp.bitwise_and(turns, NPHI - 1) - NPHI // 2
    angle = centred.astype(jnp.float32) * (2.0 * math.pi / NPHI)
    square = angle * angle
    total = jnp.full_like(square, COSINE[-1])
    for weight in COSINE[-2::-1]:
        total = total * square + weight
    return -total


def iota(shape, axis):
    return lax.broadcasted_iota(jnp.int32, shape, axis)


def dot(a, b):
    return jnp.dot(a, b, preferred_element_type=jnp.float32)


def dot_rows(a, b, precision=None):
    return lax.dot_general(
        a, b, (((0,), (0,)), ((), ())), preferred_element_type=jnp.float32, precision=precision
    )


def ones_where(mask):
    return jnp.where(mask, 1.0, 0.0).astype(jnp.bfloat16)


def list_ranks(codes):
    entries = codes.shape[0]
    listed = codes >= 0
    below = ones_where(iota((entries, entries), 0) > iota((entries, entries), 1))
    rank = dot(below, ones_where(listed))
    return jnp.where(listed, rank, UNLISTED)


def payload_places():
    return iota((1, BANDS * ROWS), 1) % ROWS


def choose_cycles(codes, cycles):
    rank = list_ranks(codes)
    entries = codes.shape[0]
    source = ones_where(iota((entries, BANDS), 0) // 2 == iota((entries, BANDS), 1))
    both = lax.dot_general(
        source,
        cycles.astype(jnp.float32).astype(jnp.bfloat16),
        (((1,), (1,)), ((), ())),
        preferred_element_type=jnp.float32,
    )
    slot = lax.shift_right_arithmetic(codes, 12)
    cycle = jnp.where(slot == 0, both[:, 0:1], jnp.where(slot == 1, both[:, 1:2], both[:, 2:3]))
    width = BANDS * ROWS
    spread = ones_where(iota((BANDS, width), 1) // ROWS == iota((BANDS, width), 0))
    rank_wide = dot(rank.astype(jnp.bfloat16), spread)
    cycle_wide = dot(cycle.astype(jnp.bfloat16), spread)
    half = payload_places() % 2
    chosen = []
    for group in range(4):
        wanted = (4 * half + group).astype(jnp.float32)
        chosen.append(
            jnp.sum(jnp.where(rank_wide == wanted, cycle_wide, 0.0), 0, keepdims=True)
        )
    return chosen


def payload_masks(chosen):
    width = BANDS * ROWS
    part_of = payload_places() // 2
    rows = [
        jnp.where(part_of == part, chosen[group], -1.0) for part in range(2) for group in range(4)
    ]
    targets = jnp.transpose(jnp.concatenate(rows, 0))
    cycle = iota((width, 128), 1).astype(jnp.float32)
    return [ones_where(cycle == targets[:, place : place + 1]) for place in range(len(rows))]


def payload_waves(coeff, psi_table):
    lane_group = iota((BANDS, 128), 1) // NPSI
    pieces = []
    for part in range(2):
        waves = dot_rows(coeff, psi_table[part], lax.Precision.HIGHEST)
        for group in range(4):
            pieces.append(jnp.where(lane_group == group, waves, 0.0).astype(jnp.bfloat16))
    return jnp.concatenate(pieces, 0)


def own_blocks(codes, owner):
    rank = list_ranks(codes)
    entries = codes.shape[0]
    mine = iota((entries, BANDS), 1) == owner
    rank_col = jnp.sum(jnp.where(mine, rank, 0.0), 1, keepdims=True)
    start = jnp.bitwise_and(codes, NPHI - 1).astype(jnp.float32)
    start_col = jnp.sum(jnp.where(mine, start, 0.0), 1, keepdims=True)
    name = (iota((entries, 128), 0) + 1).astype(jnp.float32)
    lanes = iota((entries, 128), 1).astype(jnp.float32)
    picked = rank_col == lanes
    name_row = jnp.sum(jnp.where(picked, name, 0.0), 0, keepdims=True) - 1.0
    start_row = jnp.sum(jnp.where(picked, start_col, 0.0), 0, keepdims=True)
    rows = LISTED * NPSI
    of_row = iota((rows, 128), 0) // NPSI == iota((rows, 128), 1)
    name_col = jnp.sum(jnp.where(of_row, name_row, 0.0), 1, keepdims=True).astype(jnp.int32)
    keys = name_col * NPSI + iota((rows, 1), 0) % NPSI
    rows = LISTED * BLOCK_PHI
    of_row = iota((rows, 128), 0) // BLOCK_PHI == iota((rows, 128), 1)
    first = jnp.sum(jnp.where(of_row, start_row, 0.0), 1, keepdims=True).astype(jnp.int32)
    columns = first + iota((rows, 1), 0) % BLOCK_PHI
    return keys, columns


def block_cells(received, cos_phase, sin_phase, scale):
    width = BANDS * ROWS
    lane_group = iota((BANDS, 128), 1) // NPSI
    halves = []
    for half in range(2):
        total = None
        for part, phase in enumerate((cos_phase, sin_phase)):
            pick = ones_where(
                iota((BANDS, width), 1) == iota((BANDS, width), 0) * ROWS + (2 * part + half)
            )
            rows = dot(pick, received)
            for group in range(4):
                first = (4 * half + group) * BLOCK_PHI
                piece = jnp.where(lane_group == group, rows, 0.0).astype(jnp.bfloat16)
                term = dot(phase[first : first + BLOCK_PHI], piece)
                total = term if total is None else total + term
        halves.append((total * scale).astype(jnp.bfloat16))
    return jnp.concatenate(halves, 1)


def blend_masks(keys, block, cell_psi):
    base = block * NPSI
    low = ones_where(keys == base + cell_psi)
    high = ones_where(keys == base + jnp.bitwise_and(cell_psi + 1, NPSI - 1))
    return low, high


def blend_weights(cell_phi, frac_phi, frac_psi):
    places = iota((BLOCK_PHI, cell_phi.shape[1]), 0)
    weight = jnp.where(places == cell_phi, 1.0 - frac_phi, 0.0)
    weight = jnp.where(places == cell_phi + 1, frac_phi, weight)
    return weight * (1.0 - frac_psi), weight * frac_psi


def signal_kernel(
    bands,
    dets,
    scale,
    beam_ref,
    panel_ref,
    sky_in,
    psi_in,
    codes_in,
    cycles_in,
    orders_in,
    block_in,
    phi_in,
    cell_in,
    frac_in,
    out_ref,
    beams,
    panel,
    part,
    parts,
    coeff,
    hot_ref,
    low_ref,
    high_ref,
    low_weight,
    high_weight,
    keys_ref,
    cos_ref,
    sin_ref,
    payload,
    received,
    sky_ref,
    psi_ref,
    codes_ref,
    cycles_ref,
    orders_ref,
    block_ref,
    phi_ref,
    cell_ref,
    frac_ref,
    in_sem,
    own_sem,
    send_sem,
    recv_sem,
    out_sem,
    all_sem,
):
    me = lax.axis_index("det")
    owner = lax.axis_index("band")
    comps, span = beams.shape[1], beams.shape[4]
    rows = 2 * dets
    peers = [lax.rem(me + step, dets) for step in range(dets)]
    barrier = pltpu.get_barrier_semaphore()

    def far_first(act):
        around = LINE // 2
        shifts = [
            around + (turn // 2 if turn % 2 == 0 else -(turn + 1) // 2)
            for turn in range(bands // LINE)
        ]
        line = lax.rem(owner, LINE)
        column = owner // LINE
        for shift in [bands // (2 * LINE) + value - around for value in shifts]:
            first = lax.rem(column + shift, bands // LINE) * LINE

            def one(step, carry):
                act(first + lax.rem(line + step, LINE))
                return carry

            if shift == 0:
                lax.fori_loop(1, LINE, one, 0)
            else:
                lax.fori_loop(around, around + LINE, one, 0, unroll=4)

    def greet(peer):
        pl.semaphore_signal(barrier, inc=1, device_id={"band": peer}, device_id_type=MESH)

    far_first(greet)
    for step in range(1, dets):
        pl.semaphore_signal(
            barrier, inc=1, device_id={"det": peers[step]}, device_id_type=MESH
        )
    staged = [
        (codes_in, codes_ref),
        (cycles_in, cycles_ref),
        (orders_in, orders_ref),
        (sky_in, sky_ref),
        (psi_in, psi_ref),
        (block_in, block_ref),
        (phi_in, phi_ref),
        (cell_in, cell_ref),
        (frac_in, frac_ref),
    ]
    loads = [
        pltpu.make_async_copy(source, target, in_sem.at[place])
        for place, (source, target) in enumerate(staged)
    ]
    for load in loads:
        load.start()
    own_panel = pltpu.make_async_copy(panel_ref, panel, own_sem.at[0])
    own_panel.start()

    shared = span // 2
    core = lax.rem(owner, 2)
    partner = owner + 1 - 2 * core
    share = pl.ds(pl.multiple_of(core * shared, shared), shared)

    def columns(det, orders):
        first = pl.multiple_of(det * span + core * shared, shared)
        return beam_ref.at[:, orders, :, pl.ds(first, shared)]

    own_columns = beam_ref.at[:, :, :, pl.ds(pl.multiple_of(me * span, span), span)]
    own_beams = pltpu.make_async_copy(own_columns, beams.at[me], own_sem.at[1])
    own_beams.start()
    for load in loads:
        load.wait()
    chosen = choose_cycles(codes_ref[...], cycles_ref[...])
    for place, hot in enumerate(payload_masks(chosen)):
        hot_ref[:, place * 128 : place * 128 + 128] = hot
    keys, places = own_blocks(codes_ref[...], owner)
    keys_ref[...] = jnp.broadcast_to(keys, keys_ref.shape)
    pl.semaphore_wait(barrier, bands - 1 + dets - 1)

    def remote(stage, step, source, target):
        return pltpu.make_async_remote_copy(
            src_ref=source,
            dst_ref=target,
            send_sem=send_sem.at[stage, step],
            recv_sem=recv_sem.at[stage, step],
            device_id={"det": peers[step]},
            device_id_type=MESH,
        )

    cuts = [
        pl.ds(first, last - first) for first, last in zip(ORDER_CUTS[:-1], ORDER_CUTS[1:])
    ]
    beam_sends = [
        [
            remote(
                stage, step, columns(peers[step], orders), beams.at[me, :, orders, :, share]
            )
            for step in range(1, dets)
        ]
        for stage, orders in enumerate(cuts)
    ]
    for copy in [copy for stage in beam_sends for copy in stage]:
        copy.start()
    turns = places * orders_ref[...]
    cos_ref[...] = cosine_of_turns(turns).astype(jnp.bfloat16)
    sin_ref[...] = cosine_of_turns(turns + NPHI // 4).astype(jnp.bfloat16)
    own_panel.wait()
    own_beams.wait()
    real_row = iota((rows, span), 0) % 2 == 0
    direct, crossed = [], []
    for comp in range(comps):
        first = jnp.broadcast_to(sky_ref[2 * comp], (rows, span))
        direct.append(jnp.where(real_row, first, -first))
        crossed.append(jnp.broadcast_to(sky_ref[2 * comp + 1], (rows, span)))

    def one_order(order, carry):
        mixed = jnp.zeros((rows, span), jnp.float32)
        for comp in range(comps):
            values = jnp.concatenate(
                [beams[det, comp, order].astype(jnp.float32) for det in range(dets)], 0
            )
            swapped = jnp.where(
                real_row, pltpu.roll(values, rows - 1, 0), pltpu.roll(values, 1, 0)
            )
            mixed = mixed + direct[comp] * values + crossed[comp] * swapped
        sums = dot(mixed.astype(jnp.bfloat16), panel[order])
        for det in range(dets):
            part[det, order] = sums[2 * det : 2 * det + 2]
        return carry

    def hand_over(stage):
        copies = []
        for step in range(1, dets):
            beam_sends[stage][step - 1].wait()
            place = beams.at[peers[dets - step], :, cuts[stage], :, share]
            copy = pltpu.make_async_remote_copy(
                src_ref=place,
                dst_ref=place,
                send_sem=send_sem.at[2 * len(cuts) + stage, step],
                recv_sem=recv_sem.at[2 * len(cuts) + stage, step],
                device_id={"band": partner},
                device_id_type=MESH,
            )
            copy.start()
            copies.append(copy)
        return copies

    sums_sends = []
    handed = hand_over(0)
    for stage, orders in enumerate(cuts):
        ahead = hand_over(stage + 1) if stage + 1 < len(cuts) else []
        for copy in handed:
            copy.wait()
        handed = ahead
        lax.fori_loop(ORDER_CUTS[stage], ORDER_CUTS[stage + 1], one_order, 0)
        for step in range(1, dets):
            copy = remote(
                len(cuts) + stage, step, part.at[peers[step], orders], parts.at[me, orders]
            )
            copy.start()
            sums_sends.append(copy)
    for copy in sums_sends:
        copy.wait()
    coeff[...] = jnp.zeros_like(coeff)
    for order in range(MPRIME):
        total = part[me, order]
        for step in range(1, dets):
            total = total + parts[peers[step], order]
        coeff[2 * order : 2 * order + 2, :] = total
    picked = dot(hot_ref[...], payload_waves(coeff[...], psi_ref))
    payload[...] = picked.astype(jnp.bfloat16).reshape(payload.shape)
    own = pltpu.make_async_copy(payload.at[owner], received.at[owner], own_sem.at[2])
    own.start()

    def send(peer):
        pltpu.make_async_remote_copy(
            src_ref=payload.at[peer],
            dst_ref=received.at[owner],
            send_sem=out_sem,
            recv_sem=all_sem,
            device_id={"band": peer},
            device_id_type=MESH,
        ).start()

    far_first(send)
    keys = keys_ref[:, 0:1]
    pieces = [
        slice(first, first + CHUNK) for first in range(0, block_ref.shape[1], CHUNK)
    ]
    for piece in pieces:
        low, high = blend_masks(keys, block_ref[:, piece], cell_ref[:, piece])
        low_ref[:, piece] = low
        high_ref[:, piece] = high
        low_part, high_part = blend_weights(
            phi_ref[:, piece], frac_ref[0, :, piece], frac_ref[1, :, piece]
        )
        low_weight[:, piece] = low_part
        high_weight[:, piece] = high_part
    own.wait()
    others = pl.ds(0, bands - 1)
    everything = pltpu.make_async_remote_copy(
        src_ref=payload.at[others],
        dst_ref=received.at[others],
        send_sem=out_sem,
        recv_sem=all_sem,
        device_id={"band": owner},
        device_id_type=MESH,
    )
    everything.wait_recv()
    cells = block_cells(
        received[...].reshape(BANDS * ROWS, 128), cos_ref, sin_ref, scale
    )
    for piece in pieces:
        value = low_weight[:, piece] * dot(cells, low_ref[:, piece])
        value = value + high_weight[:, piece] * dot(cells, high_ref[:, piece])
        out_ref[:, piece] = jnp.sum(value, 0, keepdims=True)
    everything.wait_send()


def per_device(
    sky_coeffs,
    beam_coeffs,
    wigner_panel,
    m_values,
    cycle_table,
    send_lists,
    sample_block,
    sample_phi,
    sample_psi,
    sample_frac,
):
    orders_all = m_values.shape[0]
    scale = 2.0 / math.sqrt(orders_all * MPRIME)
    comps, span = sky_coeffs.shape[0], sky_coeffs.shape[3]
    cycles = wigner_panel.shape[3]
    beams = jnp.transpose(beam_coeffs[0], (0, 2, 1, 3))
    dets = beams.shape[3] // span
    samples = sample_block.shape[1]
    codes = jnp.transpose(send_lists[0], (0, 2, 1)).reshape(2 * BANDS, BANDS)
    small = [
        sky_coeffs.reshape(2 * comps, 1, span),
        jnp.asarray(psi_matrices()),
        codes,
        cycle_table.T,
        m_values.reshape(1, orders_all),
        sample_block,
        sample_phi,
        sample_psi,
        sample_frac,
    ]
    return pl.pallas_call(
        functools.partial(signal_kernel, BANDS, dets, scale),
        out_shape=jax.ShapeDtypeStruct((1, samples), jnp.float32),
        in_specs=[pl.BlockSpec(memory_space=pl.ANY)] * (2 + len(small)),
        out_specs=pl.BlockSpec(memory_space=pltpu.VMEM),
        scratch_shapes=[
            pltpu.VMEM((dets, comps, MPRIME, 2, span), jnp.bfloat16),
            pltpu.VMEM((MPRIME, span, cycles), jnp.bfloat16),
            pltpu.VMEM((dets, MPRIME, 2, cycles), jnp.float32),
            pltpu.VMEM((dets, MPRIME, 2, cycles), jnp.float32),
            pltpu.VMEM((ORDERS_PAD, cycles), jnp.float32),
            pltpu.VMEM((BANDS * ROWS, 8 * cycles), jnp.bfloat16),
            pltpu.VMEM((LISTED * NPSI, samples), jnp.bfloat16),
            pltpu.VMEM((LISTED * NPSI, samples), jnp.bfloat16),
            pltpu.VMEM((BLOCK_PHI, samples), jnp.float32),
            pltpu.VMEM((BLOCK_PHI, samples), jnp.float32),
            pltpu.VMEM((LISTED * NPSI, 128), jnp.int32),
            pltpu.VMEM((LISTED * BLOCK_PHI, orders_all), jnp.bfloat16),
            pltpu.VMEM((LISTED * BLOCK_PHI, orders_all), jnp.bfloat16),
            pltpu.VMEM((BANDS, ROWS, 128), jnp.bfloat16),
            pltpu.VMEM((BANDS, ROWS, 128), jnp.bfloat16),
        ]
        + [pltpu.VMEM(array.shape, array.dtype) for array in small]
        + [
            pltpu.SemaphoreType.DMA((len(small),)),
            pltpu.SemaphoreType.DMA((3,)),
            pltpu.SemaphoreType.DMA((3 * len(ORDER_CUTS) - 3, dets)),
            pltpu.SemaphoreType.DMA((3 * len(ORDER_CUTS) - 3, dets)),
            pltpu.SemaphoreType.DMA,
            pltpu.SemaphoreType.DMA,
        ],
        compiler_params=pltpu.CompilerParams(collective_id=0, has_side_effects=True),
    )(beams, wigner_panel[0], *small)


def solution(mesh):
    return jax.shard_map(
        per_device,
        mesh=mesh,
        in_specs=(
            P(None, None, "band", "det"),
            P("det", None, None, None, None),
            P("band", None, "det", None),
            P(),
            P(),
            P("det", None, None, None),
            P("det", "band"),
            P("det", "band"),
            P("det", "band"),
            P(None, "det", "band"),
        ),
        out_specs=P("det", "band"),
        check_vma=False,
    )
```

```python
import functools
import math

import jax
import jax.numpy as jnp
import numpy as np
from jax import lax
from jax.experimental import pallas as pl
from jax.experimental.pallas import tpu as pltpu
from jax.sharding import PartitionSpec as P

BMAX = 8
MPRIME = 17
NPSI = 32
NPHI = 4096
BLOCK_PHI = 128
BANDS = 128
LISTED = 8
ROWS = 4
ORDERS_PAD = 40
CHUNK = 512
LINE = 16
ORDER_CUTS = (0, 6, 12, 17)
UNLISTED = 200.0
MESH = pl.DeviceIdType.MESH


def psi_matrices():
    orders = np.arange(MPRIME) - BMAX
    cells = np.arange(128) % NPSI
    angle = 2.0 * math.pi / NPSI * ((orders[:, None] * cells[None, :]) % NPSI)
    cos_psi, sin_psi = np.cos(angle), np.sin(angle)
    table = np.zeros((2, ORDERS_PAD, 128), np.float32)
    table[0, 0 : 2 * MPRIME : 2] = cos_psi
    table[0, 1 : 2 * MPRIME : 2] = -sin_psi
    table[1, 0 : 2 * MPRIME : 2] = sin_psi
    table[1, 1 : 2 * MPRIME : 2] = cos_psi
    return table


def cosine_weights():
    nodes = np.cos(math.pi * (np.arange(64) + 0.5) / 64)
    top = math.pi**2
    squares = (nodes + 1.0) * top / 2
    fit = np.polynomial.chebyshev.Chebyshev.fit(squares, np.cos(np.sqrt(squares)), 8, domain=[0, top])
    weights = fit.convert(kind=np.polynomial.Polynomial).coef
    return [float(w) for w in weights]


COSINE = cosine_weights()


def cosine_of_turns(turns):
    centred = jnp.bitwise_and(turns, NPHI - 1) - NPHI // 2
    angle = centred.astype(jnp.float32) * (2.0 * math.pi / NPHI)
    square = angle * angle
    total = jnp.full_like(square, COSINE[-1])
    for weight in COSINE[-2::-1]:
        total = total * square + weight
    return -total


def iota(shape, axis):
    return lax.broadcasted_iota(jnp.int32, shape, axis)


def dot(a, b):
    return jnp.dot(a, b, preferred_element_type=jnp.float32)


def dot_rows(a, b, precision=None):
    return lax.dot_general(
        a, b, (((0,), (0,)), ((), ())), preferred_element_type=jnp.float32, precision=precision
    )


def ones_where(mask):
    return jnp.where(mask, 1.0, 0.0).astype(jnp.bfloat16)


def list_ranks(codes):
    entries = codes.shape[0]
    listed = codes >= 0
    below = ones_where(iota((entries, entries), 0) > iota((entries, entries), 1))
    rank = dot(below, ones_where(listed))
    return jnp.where(listed, rank, UNLISTED)


def payload_places():
    return iota((1, BANDS * ROWS), 1) % ROWS


def choose_cycles(codes, cycles):
    rank = list_ranks(codes)
    entries = codes.shape[0]
    source = ones_where(iota((entries, BANDS), 0) // 2 == iota((entries, BANDS), 1))
    both = lax.dot_general(
        source,
        cycles.astype(jnp.float32).astype(jnp.bfloat16),
        (((1,), (1,)), ((), ())),
        preferred_element_type=jnp.float32,
    )
    slot = lax.shift_right_arithmetic(codes, 12)
    cycle = jnp.where(slot == 0, both[:, 0:1], jnp.where(slot == 1, both[:, 1:2], both[:, 2:3]))
    width = BANDS * ROWS
    spread = ones_where(iota((BANDS, width), 1) // ROWS == iota((BANDS, width), 0))
    rank_wide = dot(rank.astype(jnp.bfloat16), spread)
    cycle_wide = dot(cycle.astype(jnp.bfloat16), spread)
    half = payload_places() % 2
    chosen = []
    for group in range(4):
        wanted = (4 * half + group).astype(jnp.float32)
        chosen.append(
            jnp.sum(jnp.where(rank_wide == wanted, cycle_wide, 0.0), 0, keepdims=True)
        )
    return chosen


def payload_masks(chosen):
    width = BANDS * ROWS
    part_of = payload_places() // 2
    rows = [
        jnp.where(part_of == part, chosen[group], -1.0) for part in range(2) for group in range(4)
    ]
    targets = jnp.transpose(jnp.concatenate(rows, 0))
    cycle = iota((width, 128), 1).astype(jnp.float32)
    return [ones_where(cycle == targets[:, place : place + 1]) for place in range(len(rows))]


def payload_waves(coeff, psi_table):
    lane_group = iota((BANDS, 128), 1) // NPSI
    pieces = []
    for part in range(2):
        waves = dot_rows(coeff, psi_table[part], lax.Precision.HIGHEST)
        for group in range(4):
            pieces.append(jnp.where(lane_group == group, waves, 0.0).astype(jnp.bfloat16))
    return jnp.concatenate(pieces, 0)


def own_blocks(codes, owner):
    rank = list_ranks(codes)
    entries = codes.shape[0]
    mine = iota((entries, BANDS), 1) == owner
    rank_col = jnp.sum(jnp.where(mine, rank, 0.0), 1, keepdims=True)
    start = jnp.bitwise_and(codes, NPHI - 1).astype(jnp.float32)
    start_col = jnp.sum(jnp.where(mine, start, 0.0), 1, keepdims=True)
    name = (iota((entries, 128), 0) + 1).astype(jnp.float32)
    lanes = iota((entries, 128), 1).astype(jnp.float32)
    picked = rank_col == lanes
    name_row = jnp.sum(jnp.where(picked, name, 0.0), 0, keepdims=True) - 1.0
    start_row = jnp.sum(jnp.where(picked, start_col, 0.0), 0, keepdims=True)
    rows = LISTED * NPSI
    of_row = iota((rows, 128), 0) // NPSI == iota((rows, 128), 1)
    name_col = jnp.sum(jnp.where(of_row, name_row, 0.0), 1, keepdims=True).astype(jnp.int32)
    keys = name_col * NPSI + iota((rows, 1), 0) % NPSI
    rows = LISTED * BLOCK_PHI
    of_row = iota((rows, 128), 0) // BLOCK_PHI == iota((rows, 128), 1)
    first = jnp.sum(jnp.where(of_row, start_row, 0.0), 1, keepdims=True).astype(jnp.int32)
    columns = first + iota((rows, 1), 0) % BLOCK_PHI
    return keys, columns


def block_cells(received, cos_phase, sin_phase, scale):
    width = BANDS * ROWS
    lane_group = iota((BANDS, 128), 1) // NPSI
    halves = []
    for half in range(2):
        total = None
        for part, phase in enumerate((cos_phase, sin_phase)):
            pick = ones_where(
                iota((BANDS, width), 1) == iota((BANDS, width), 0) * ROWS + (2 * part + half)
            )
            rows = dot(pick, received)
            for group in range(4):
                first = (4 * half + group) * BLOCK_PHI
                piece = jnp.where(lane_group == group, rows, 0.0).astype(jnp.bfloat16)
                term = dot(phase[first : first + BLOCK_PHI], piece)
                total = term if total is None else total + term
        halves.append((total * scale).astype(jnp.bfloat16))
    return jnp.concatenate(halves, 1)


def blend_masks(keys, block, cell_psi):
    base = block * NPSI
    low = ones_where(keys == base + cell_psi)
    high = ones_where(keys == base + jnp.bitwise_and(cell_psi + 1, NPSI - 1))
    return low, high


def blend_weights(cell_phi, frac_phi, frac_psi):
    places = iota((BLOCK_PHI, cell_phi.shape[1]), 0)
    weight = jnp.where(places == cell_phi, 1.0 - frac_phi, 0.0)
    weight = jnp.where(places == cell_phi + 1, frac_phi, weight)
    return weight * (1.0 - frac_psi), weight * frac_psi


def signal_kernel(
    bands,
    dets,
    scale,
    beam_ref,
    panel_ref,
    sky_in,
    psi_in,
    codes_in,
    cycles_in,
    orders_in,
    block_in,
    phi_in,
    cell_in,
    frac_in,
    out_ref,
    beams,
    panel,
    part,
    parts,
    coeff,
    hot_ref,
    low_ref,
    high_ref,
    low_weight,
    high_weight,
    keys_ref,
    cos_ref,
    sin_ref,
    payload,
    received,
    sky_ref,
    psi_ref,
    codes_ref,
    cycles_ref,
    orders_ref,
    block_ref,
    phi_ref,
    cell_ref,
    frac_ref,
    in_sem,
    own_sem,
    send_sem,
    recv_sem,
    out_sem,
    all_sem,
):
    me = lax.axis_index("det")
    owner = lax.axis_index("band")
    comps, span = beams.shape[1], beams.shape[4]
    rows = 2 * dets
    peers = [lax.rem(me + step, dets) for step in range(dets)]
    barrier = pltpu.get_barrier_semaphore()

    def far_first(act):
        around = LINE // 2
        shifts = [
            around + (turn // 2 if turn % 2 == 0 else -(turn + 1) // 2)
            for turn in range(bands // LINE)
        ]
        line = lax.rem(owner, LINE)
        column = owner // LINE
        for shift in [bands // (2 * LINE) + value - around for value in shifts]:
            first = lax.rem(column + shift, bands // LINE) * LINE

            def one(step, carry):
                act(first + lax.rem(line + step, LINE))
                return carry

            if shift == 0:
                lax.fori_loop(1, LINE, one, 0)
            else:
                lax.fori_loop(around, around + LINE, one, 0, unroll=4)

    def greet(peer):
        pl.semaphore_signal(barrier, inc=1, device_id={"band": peer}, device_id_type=MESH)

    far_first(greet)
    for step in range(1, dets):
        pl.semaphore_signal(
            barrier, inc=1, device_id={"det": peers[step]}, device_id_type=MESH
        )
    staged = [
        (codes_in, codes_ref),
        (cycles_in, cycles_ref),
        (orders_in, orders_ref),
        (sky_in, sky_ref),
        (psi_in, psi_ref),
        (block_in, block_ref),
        (phi_in, phi_ref),
        (cell_in, cell_ref),
        (frac_in, frac_ref),
    ]
    loads = [
        pltpu.make_async_copy(source, target, in_sem.at[place])
        for place, (source, target) in enumerate(staged)
    ]
    for load in loads:
        load.start()
    own_panel = pltpu.make_async_copy(panel_ref, panel, own_sem.at[0])
    own_panel.start()

    def columns(det, orders):
        return beam_ref.at[:, orders, :, pl.ds(pl.multiple_of(det * span, span), span)]

    every_order = pl.ds(0, MPRIME)
    own_beams = pltpu.make_async_copy(columns(me, every_order), beams.at[me], own_sem.at[1])
    own_beams.start()
    for load in loads:
        load.wait()
    chosen = choose_cycles(codes_ref[...], cycles_ref[...])
    for place, hot in enumerate(payload_masks(chosen)):
        hot_ref[:, place * 128 : place * 128 + 128] = hot
    keys, places = own_blocks(codes_ref[...], owner)
    keys_ref[...] = jnp.broadcast_to(keys, keys_ref.shape)
    pl.semaphore_wait(barrier, bands - 1 + dets - 1)

    def remote(stage, step, source, target):
        return pltpu.make_async_remote_copy(
            src_ref=source,
            dst_ref=target,
            send_sem=send_sem.at[stage, step],
            recv_sem=recv_sem.at[stage, step],
            device_id={"det": peers[step]},
            device_id_type=MESH,
        )

    cuts = [
        pl.ds(first, last - first) for first, last in zip(ORDER_CUTS[:-1], ORDER_CUTS[1:])
    ]
    beam_sends = [
        [
            remote(
                stage, step, columns(peers[step], orders), beams.at[me, :, orders]
            )
            for step in range(1, dets)
        ]
        for stage, orders in enumerate(cuts)
    ]
    for copy in [copy for stage in beam_sends for copy in stage]:
        copy.start()
    turns = places * orders_ref[...]
    cos_ref[...] = cosine_of_turns(turns).astype(jnp.bfloat16)
    sin_ref[...] = cosine_of_turns(turns + NPHI // 4).astype(jnp.bfloat16)
    own_panel.wait()
    own_beams.wait()
    real_row = iota((rows, span), 0) % 2 == 0
    direct, crossed = [], []
    for comp in range(comps):
        first = jnp.broadcast_to(sky_ref[2 * comp], (rows, span))
        direct.append(jnp.where(real_row, first, -first))
        crossed.append(jnp.broadcast_to(sky_ref[2 * comp + 1], (rows, span)))

    def one_order(order, carry):
        mixed = jnp.zeros((rows, span), jnp.float32)
        for comp in range(comps):
            values = jnp.concatenate(
                [beams[det, comp, order].astype(jnp.float32) for det in range(dets)], 0
            )
            swapped = jnp.where(
                real_row, pltpu.roll(values, rows - 1, 0), pltpu.roll(values, 1, 0)
            )
            mixed = mixed + direct[comp] * values + crossed[comp] * swapped
        sums = dot(mixed.astype(jnp.bfloat16), panel[order])
        for det in range(dets):
            part[det, order] = sums[2 * det : 2 * det + 2]
        return carry

    sums_sends = []
    for stage, orders in enumerate(cuts):
        for copy in beam_sends[stage]:
            copy.wait()
        lax.fori_loop(ORDER_CUTS[stage], ORDER_CUTS[stage + 1], one_order, 0, unroll=True)
        for step in range(1, dets):
            copy = remote(
                len(cuts) + stage, step, part.at[peers[step], orders], parts.at[me, orders]
            )
            copy.start()
            sums_sends.append(copy)
    for copy in sums_sends:
        copy.wait()
    coeff[...] = jnp.zeros_like(coeff)
    for order in range(MPRIME):
        total = part[me, order]
        for step in range(1, dets):
            total = total + parts[peers[step], order]
        coeff[2 * order : 2 * order + 2, :] = total
    picked = dot(hot_ref[...], payload_waves(coeff[...], psi_ref))
    payload[...] = picked.astype(jnp.bfloat16).reshape(payload.shape)
    own = pltpu.make_async_copy(payload.at[owner], received.at[owner], own_sem.at[2])
    own.start()

    def send(peer):
        pltpu.make_async_remote_copy(
            src_ref=payload.at[peer],
            dst_ref=received.at[owner],
            send_sem=out_sem,
            recv_sem=all_sem,
            device_id={"band": peer},
            device_id_type=MESH,
        ).start()

    far_first(send)
    keys = keys_ref[:, 0:1]
    pieces = [
        slice(first, first + CHUNK) for first in range(0, block_ref.shape[1], CHUNK)
    ]
    for piece in pieces:
        low, high = blend_masks(keys, block_ref[:, piece], cell_ref[:, piece])
        low_ref[:, piece] = low
        high_ref[:, piece] = high
        low_part, high_part = blend_weights(
            phi_ref[:, piece], frac_ref[0, :, piece], frac_ref[1, :, piece]
        )
        low_weight[:, piece] = low_part
        high_weight[:, piece] = high_part
    own.wait()
    others = pl.ds(0, bands - 1)
    everything = pltpu.make_async_remote_copy(
        src_ref=payload.at[others],
        dst_ref=received.at[others],
        send_sem=out_sem,
        recv_sem=all_sem,
        device_id={"band": owner},
        device_id_type=MESH,
    )
    everything.wait_recv()
    cells = block_cells(
        received[...].reshape(BANDS * ROWS, 128), cos_ref, sin_ref, scale
    )
    for piece in pieces:
        value = low_weight[:, piece] * dot(cells, low_ref[:, piece])
        value = value + high_weight[:, piece] * dot(cells, high_ref[:, piece])
        out_ref[:, piece] = jnp.sum(value, 0, keepdims=True)
    everything.wait_send()


def per_device(
    sky_coeffs,
    beam_coeffs,
    wigner_panel,
    m_values,
    cycle_table,
    send_lists,
    sample_block,
    sample_phi,
    sample_psi,
    sample_frac,
):
    orders_all = m_values.shape[0]
    scale = 2.0 / math.sqrt(orders_all * MPRIME)
    comps, span = sky_coeffs.shape[0], sky_coeffs.shape[3]
    cycles = wigner_panel.shape[3]
    beams = jnp.transpose(beam_coeffs[0], (0, 2, 1, 3))
    dets = beams.shape[3] // span
    samples = sample_block.shape[1]
    codes = jnp.transpose(send_lists[0], (0, 2, 1)).reshape(2 * BANDS, BANDS)
    small = [
        sky_coeffs.reshape(2 * comps, 1, span),
        jnp.asarray(psi_matrices()),
        codes,
        cycle_table.T,
        m_values.reshape(1, orders_all),
        sample_block,
        sample_phi,
        sample_psi,
        sample_frac,
    ]
    return pl.pallas_call(
        functools.partial(signal_kernel, BANDS, dets, scale),
        out_shape=jax.ShapeDtypeStruct((1, samples), jnp.float32),
        in_specs=[pl.BlockSpec(memory_space=pl.ANY)] * (2 + len(small)),
        out_specs=pl.BlockSpec(memory_space=pltpu.VMEM),
        scratch_shapes=[
            pltpu.VMEM((dets, comps, MPRIME, 2, span), jnp.bfloat16),
            pltpu.VMEM((MPRIME, span, cycles), jnp.bfloat16),
            pltpu.VMEM((dets, MPRIME, 2, cycles), jnp.float32),
            pltpu.VMEM((dets, MPRIME, 2, cycles), jnp.float32),
            pltpu.VMEM((ORDERS_PAD, cycles), jnp.float32),
            pltpu.VMEM((BANDS * ROWS, 8 * cycles), jnp.bfloat16),
            pltpu.VMEM((LISTED * NPSI, samples), jnp.bfloat16),
            pltpu.VMEM((LISTED * NPSI, samples), jnp.bfloat16),
            pltpu.VMEM((BLOCK_PHI, samples), jnp.float32),
            pltpu.VMEM((BLOCK_PHI, samples), jnp.float32),
            pltpu.VMEM((LISTED * NPSI, 128), jnp.int32),
            pltpu.VMEM((LISTED * BLOCK_PHI, orders_all), jnp.bfloat16),
            pltpu.VMEM((LISTED * BLOCK_PHI, orders_all), jnp.bfloat16),
            pltpu.VMEM((BANDS, ROWS, 128), jnp.bfloat16),
            pltpu.VMEM((BANDS, ROWS, 128), jnp.bfloat16),
        ]
        + [pltpu.VMEM(array.shape, array.dtype) for array in small]
        + [
            pltpu.SemaphoreType.DMA((len(small),)),
            pltpu.SemaphoreType.DMA((3,)),
            pltpu.SemaphoreType.DMA((2 * len(ORDER_CUTS) - 2, dets)),
            pltpu.SemaphoreType.DMA((2 * len(ORDER_CUTS) - 2, dets)),
            pltpu.SemaphoreType.DMA,
            pltpu.SemaphoreType.DMA,
        ],
        compiler_params=pltpu.CompilerParams(collective_id=0, has_side_effects=True),
    )(beams, wigner_panel[0], *small)


def solution(mesh):
    return jax.shard_map(
        per_device,
        mesh=mesh,
        in_specs=(
            P(None, None, "band", "det"),
            P("det", None, None, None, None),
            P("band", None, "det", None),
            P(),
            P(),
            P("det", None, None, None),
            P("det", "band"),
            P("det", "band"),
            P("det", "band"),
            P(None, "det", "band"),
        ),
        out_specs=P("det", "band"),
        check_vma=False,
    )
```
